128 devices in a mesh: space: 32 (over y, x, core), chan: 4 (over z).
Axes of the slice: x: 4, y: 4, z: 4, core: 2. Of those that a mesh axis runs over, the one named last changes fastest.
Arguments:
- features: bfloat16 [128, 16, 256, 128], P('space', None, 'chan'), may hold values from -6 to 6
- fluid_tiles: int32 [32, 4, 8], P('space', None, 'chan'), may hold values from 0 to 1, as said below
- weight_one: bfloat16 [128, 3, 3, 3, 128], replicated, may hold values from -0.109375 to 0.109375
- weight_two: bfloat16 [128, 3, 3, 3, 128], replicated, may hold values from -0.109375 to 0.109375
- weight_three: bfloat16 [128, 3, 3, 3, 128], replicated, may hold values from -0.109375 to 0.109375
- upstream: bfloat16 [64, 8, 128, 128], P('space', None, 'chan'), may hold values from -6 to 6
Outputs:
- coarse_out: bfloat16 [64, 8, 128, 128], P('space', None, 'chan')
- grad_one: float32 [128, 3, 3, 3, 128], P('chan')
- grad_two: float32 [128, 3, 3, 3, 128], P('chan')
- grad_three: float32 [128, 3, 3, 3, 128], P('chan')
The draws below stay inside these ranges and needn't reach their ends.
Inputs may be any that keep to these rules, and one draw needn't show every extreme that they name: `fluid_tiles`: in each index of the last dimension's 2-tile groups exactly 85 tiles are fluid; all tiles of the first block along the first dimension are fluid.
All inputs are finite; a program needn't handle non-finite values.
Results may differ from the reference program's by a relative error of at most 0.012.
Values may be sent and summed in bfloat16 or wider, within the bound.
A program may use at most 128 MiB of HBM per device.

```python
import jax
import jax.numpy as jnp
from jax import lax

CHANNELS = 128
TILE_X = 4
TILE_Z = 4
TILE_Y = 32
SLAB_DEPTH = 16
TILES_Y_DEV = 2
EXTENT_X = 128
EXTENT_Y = 256
TILES_DEV = 8
ACTIVE_COL = 85
N_SPACE = 32
N_CHAN = 4


def draw_fluid_tiles(key, part):
    folded = jax.random.fold_in(key, 7)
    key_bias, key_noise = jax.random.split(folded, 2)
    device_bias = jax.random.randint(key_bias, (N_SPACE, N_CHAN), 0, 4096)
    device_bias = device_bias.at[0].set(1 << 22)
    noise = jax.random.randint(key_noise, (N_SPACE, N_CHAN, TILES_DEV), 0, 8192)
    scores = noise + device_bias[:, :, None]
    columns = jnp.transpose(scores, (1, 0, 2)).reshape(N_CHAN, N_SPACE * TILES_DEV)

    def one_column(column_scores):
        order = jnp.argsort(-column_scores, stable=True)
        ranks = jnp.argsort(order, stable=True).astype(jnp.int32)
        return (ranks < ACTIVE_COL).astype(jnp.int32)
    fluid = jax.vmap(one_column)(columns)
    shaped = fluid.reshape(N_CHAN, N_SPACE, SLAB_DEPTH // TILE_Z, TILES_Y_DEV)
    return jnp.transpose(shaped, (1, 2, 0, 3)).reshape(N_SPACE, SLAB_DEPTH // TILE_Z, N_CHAN * TILES_Y_DEV).astype(jnp.int32)


def steps_of(rng, extent, shards, least, high):
    def one(dim, parts):
        steps = jax.random.uniform(jax.random.fold_in(jax.random.fold_in(rng, 6), dim), (parts,), jnp.float32, least / len(shards), high / len(shards))
        return jnp.repeat(jnp.exp(steps), extent[dim] // parts).reshape((-1,) + (1,) * (len(extent) - dim - 1))

    factor_of = one(*shards[0])
    for cut in shards[1:]:
        factor_of = factor_of * one(*cut)
    return factor_of


def scatter_about(own_key, dims, scale, limit, cuts=(), held_as=jnp.bfloat16):
    factor_of = steps_of(own_key, dims, cuts, -0.22, 0.18) if cuts else 1.0
    array = jax.random.normal(own_key, dims, jnp.float32) * scale * factor_of
    return jnp.minimum(jnp.maximum(array, -limit), limit).astype(held_as)


def setup_inputs(seed: int = 0) -> dict:
    keys = jax.random.split(jax.random.key(seed), 7)
    features = scatter_about(keys[0], (EXTENT_X, SLAB_DEPTH, EXTENT_Y, CHANNELS), 1.0, 6.0, ((0, 32), (2, 4)))
    fluid_tiles = draw_fluid_tiles(jax.random.fold_in(keys[6], 71), 0)
    weight_one = scatter_about(keys[2], (CHANNELS, 3, 3, 3, CHANNELS), (27 * CHANNELS) ** -0.5, 0.109375)
    weight_two = scatter_about(keys[3], (CHANNELS, 3, 3, 3, CHANNELS), (27 * CHANNELS) ** -0.5, 0.109375)
    weight_three = scatter_about(keys[4], (CHANNELS, 3, 3, 3, CHANNELS), (27 * CHANNELS) ** -0.5, 0.109375)
    upstream = scatter_about(keys[5], (EXTENT_X // 2, SLAB_DEPTH // 2, EXTENT_Y // 2, CHANNELS), 1.0, 6.0, ((0, 32), (2, 4)))
    return {"features": features, "fluid_tiles": fluid_tiles, "weight_one": weight_one, "weight_two": weight_two, "weight_three": weight_three, "upstream": upstream}


NUMBERS = ('NDHWC', 'ODHWI', 'NDHWC')

def convolve(inputs, weight, stride, spread, margins):
    result = lax.conv_general_dilated(inputs.astype(jnp.float32)[None], weight.astype(jnp.float32), (stride, stride, stride), margins, rhs_dilation=(spread, spread, spread), dimension_numbers=NUMBERS, precision=lax.Precision.HIGHEST)
    return result[0]

def silu_slope(values):
    sigma = jax.nn.sigmoid(values)
    return sigma * (1.0 + values * (1.0 - sigma))

def cell_mask(fluid_tiles):
    blocks = fluid_tiles.astype(jnp.float32)
    blocks = jnp.repeat(blocks, TILE_X, axis=0)
    blocks = jnp.repeat(blocks, TILE_Z, axis=1)
    return jnp.repeat(blocks, TILE_Y, axis=2)[..., None]

def reference(features, fluid_tiles, weight_one, weight_two, weight_three, upstream):
    mask = cell_mask(fluid_tiles)
    same_edge = [(1, 1)] * 3
    wide_edge = [(2, 2)] * 3
    lower_edge = [(1, 0)] * 3
    pre_one = convolve(features, weight_one, 1, 1, same_edge)
    hidden_one = (mask * jax.nn.silu(pre_one)).astype(jnp.bfloat16)
    pre_two = convolve(hidden_one, weight_two, 1, 2, wide_edge)
    hidden_two = (mask * jax.nn.silu(pre_two)).astype(jnp.bfloat16)
    coarse = convolve(hidden_two, weight_three, 2, 1, lower_edge)
    coarse_out = coarse.astype(jnp.bfloat16)
    cotangent = upstream.astype(jnp.float32)
    _, pull_three = jax.vjp(lambda inputs, weight: convolve(inputs, weight, 2, 1, lower_edge), hidden_two.astype(jnp.float32), weight_three.astype(jnp.float32))
    back_two, grad_three = pull_three(cotangent)
    back_two = back_two.astype(jnp.bfloat16)
    slope_two = (back_two.astype(jnp.float32) * mask * silu_slope(pre_two)).astype(jnp.bfloat16)
    _, pull_two = jax.vjp(lambda inputs, weight: convolve(inputs, weight, 1, 2, wide_edge), hidden_one.astype(jnp.float32), weight_two.astype(jnp.float32))
    back_one, grad_two = pull_two(slope_two.astype(jnp.float32))
    back_one = back_one.astype(jnp.bfloat16)
    slope_one = (back_one.astype(jnp.float32) * mask * silu_slope(pre_one)).astype(jnp.bfloat16)
    _, pull_one = jax.vjp(lambda weight: convolve(features, weight, 1, 1, same_edge), weight_one.astype(jnp.float32))
    grad_one, = pull_one(slope_one.astype(jnp.float32))
    return (coarse_out, grad_one, grad_two, grad_three)
```

```python
import jax
import jax.numpy as jnp
from jax import lax
from jax.sharding import PartitionSpec as P

TILE_Z = 4
TILE_Y = 32


NUMBERS = ("NDHWC", "ODHWI", "NDHWC")


def padded(shard, sides, width):
    for axis, dim in sides:
        devices, length = (lax.axis_size(axis), shard.shape[dim])
        up = [(i, (i + 1) % devices) for i in range(devices - 1)]
        down = [(j, i) for i, j in up]
        last = lax.slice_in_dim(shard, length - width, length, axis=dim)
        leading = lax.slice_in_dim(shard, 0, width, axis=dim)
        before = lax.ppermute(last, axis, up)
        after = lax.ppermute(leading, axis, down)
        shard = jnp.concatenate([before, shard, after], axis=dim)
    return shard


def from_behind(block, axis, distance):
    devices = range(lax.axis_size(axis))
    route = [(i - distance, i) for i in devices if i - distance in devices]
    return lax.ppermute(block, axis, route)


def convolve(inputs, weight, stride, spread):
    return lax.conv_general_dilated(
        inputs,
        weight,
        (stride, stride, stride),
        "VALID",
        rhs_dilation=(spread, spread, spread),
        dimension_numbers=NUMBERS,
        preferred_element_type=jnp.float32,
    )


def flipped(weight):
    return jnp.swapaxes(weight[:, ::-1, ::-1, ::-1], 0, 4)


def tap_grads(window, grads, stride, spread):
    batch, extent_x, extent_z, extent_y, outputs = grads.shape
    inputs = window.shape[4]
    flat_grads = grads.reshape(-1, outputs)
    results = []
    for tap_x in range(3):
        for tap_z in range(3):
            for tap_y in range(3):
                begin = (0, tap_x * spread, tap_z * spread, tap_y * spread, 0)
                finish = (
                    batch,
                    begin[1] + (extent_x - 1) * stride + 1,
                    begin[2] + (extent_z - 1) * stride + 1,
                    begin[3] + (extent_y - 1) * stride + 1,
                    inputs,
                )
                piece = lax.slice(window, begin, finish, (1, stride, stride, stride, 1))
                results.append(
                    lax.dot_general(
                        flat_grads,
                        piece.reshape(-1, inputs),
                        (((0,), (0,)), ((), ())),
                        preferred_element_type=jnp.float32,
                    )
                )
    return jnp.stack(results, axis=1).reshape(outputs, 3, 3, 3, inputs)


def strided_grads(window, grads):
    extent_x, extent_z, extent_y, outputs = grads.shape
    inputs = window.shape[3]
    even = jnp.pad(window, ((0, 1), (0, 1), (0, 1), (0, 0)))
    split = even.reshape(extent_x + 1, 2, extent_z + 1, 2, extent_y + 1, 2, inputs)
    split = jnp.transpose(split, (1, 3, 5, 0, 2, 4, 6))
    flat_grads = grads.reshape(-1, outputs)
    results = []
    for tap_x in range(3):
        for tap_z in range(3):
            for tap_y in range(3):
                plane = split[tap_x % 2, tap_z % 2, tap_y % 2]
                begin = (tap_x // 2, tap_z // 2, tap_y // 2)
                piece = plane[
                    begin[0] : begin[0] + extent_x,
                    begin[1] : begin[1] + extent_z,
                    begin[2] : begin[2] + extent_y,
                ]
                results.append(
                    lax.dot_general(
                        flat_grads,
                        piece.reshape(-1, inputs),
                        (((0,), (0,)), ((), ())),
                        preferred_element_type=jnp.float32,
                    )
                )
    return jnp.stack(results, axis=1).reshape(outputs, 3, 3, 3, inputs)


def silu_slope(values):
    sigma = jax.nn.sigmoid(values)
    return sigma * (1.0 + values * (1.0 - sigma))


def cell_mask(fluid_tiles, rows, depth, length):
    blocks = fluid_tiles.reshape(depth // TILE_Z, length // TILE_Y).astype(jnp.float32)
    blocks = jnp.repeat(jnp.repeat(blocks, TILE_Z, axis=0), TILE_Y, axis=1)
    return jnp.broadcast_to(blocks[None, :, :, None], (rows, depth, length, 1))


def local(features, fluid_tiles, weight_one, weight_two, weight_three, upstream):
    rows, depth, length, chans = features.shape
    mask = cell_mask(fluid_tiles, rows, depth, length)
    with_rim = padded(features, (("space", 0), ("chan", 2)), 1)
    padded_one = jnp.pad(with_rim, ((0, 0), (1, 1), (0, 0), (0, 0)))
    pre_one = convolve(padded_one[None], weight_one, 1, 1)[0]
    hidden_one = (mask * jax.nn.silu(pre_one)).astype(jnp.bfloat16)
    rim_two = padded(hidden_one, (("space", 0), ("chan", 2)), 2)
    padded_two = jnp.pad(rim_two, ((0, 0), (2, 2), (0, 0), (0, 0)))
    pre_two = convolve(padded_two[None], weight_two, 1, 2)[0]
    hidden_two = (mask * jax.nn.silu(pre_two)).astype(jnp.bfloat16)
    before_x = from_behind(hidden_two[-1:], "space", 1)
    extended = jnp.concatenate([before_x, hidden_two], axis=0)
    before_y = from_behind(extended[:, :, -1:], "chan", 1)
    extended = jnp.concatenate([before_y, extended], axis=2)
    padded_three = jnp.pad(extended, ((0, 0), (1, 0), (0, 0), (0, 0)))
    coarse = convolve(padded_three[None], weight_three, 2, 1)[0]
    coarse_out = coarse.astype(jnp.bfloat16)
    after_x = from_behind(upstream[:1], "space", -1)
    stretched = jnp.concatenate([upstream, after_x], axis=0)
    after_y = from_behind(stretched[:, :, :1], "chan", -1)
    stretched = jnp.concatenate([stretched, after_y], axis=2)
    partial_two = lax.conv_general_dilated(
        stretched[None],
        flipped(weight_three),
        (1, 1, 1),
        [(2, 2), (2, 3), (2, 2)],
        lhs_dilation=(2, 2, 2),
        dimension_numbers=NUMBERS,
        preferred_element_type=jnp.float32,
    )[0]
    back_two = partial_two[1 : rows + 1, 1 : depth + 1, 1 : length + 1].astype(jnp.bfloat16)
    grad_three = strided_grads(padded_three, upstream)
    slope_two = (back_two.astype(jnp.float32) * mask * silu_slope(pre_two)).astype(jnp.bfloat16)
    slope_rim = padded(slope_two, (("space", 0), ("chan", 2)), 2)
    slope_pad = jnp.pad(slope_rim, ((0, 0), (2, 2), (0, 0), (0, 0)))
    back_one = convolve(slope_pad[None], flipped(weight_two), 1, 2)[0].astype(jnp.bfloat16)
    grad_two = tap_grads(padded_two[None], slope_two[None], 1, 2)
    slope_one = (back_one.astype(jnp.float32) * mask * silu_slope(pre_one)).astype(jnp.bfloat16)
    grad_one = tap_grads(padded_one[None], slope_one[None], 1, 1)
    stacked = jnp.concatenate([grad_one, grad_two, grad_three], axis=1)
    stacked = lax.psum_scatter(stacked, "chan", scatter_dimension=0, tiled=True)
    stacked = lax.psum(stacked, "space")
    grad_one, grad_two, grad_three = jnp.split(stacked, 3, axis=1)
    return (coarse_out, grad_one, grad_two, grad_three)


def solution(mesh):
    in_specs = (
        P("space", None, "chan", None),
        P("space", None, "chan"),
        P(),
        P(),
        P(),
        P("space", None, "chan", None),
    )
    out_specs = (
        P("space", None, "chan", None),
        P("chan", None, None, None, None),
        P("chan", None, None, None, None),
        P("chan", None, None, None, None),
    )
    return jax.shard_map(local, mesh=mesh, in_specs=in_specs, out_specs=out_specs, check_vma=False)
```

```python
import functools

import jax
import jax.numpy as jnp
from jax import lax
from jax.experimental import pallas as pl
from jax.experimental.pallas import tpu as pltpu
from jax.sharding import PartitionSpec as P

TILE_Z = 4
TILE_Y = 32
ROWS = 4
LENGTH = 64
DEPTH = 16
CH = 128
HALF = LENGTH // 2
CELLS = HALF * DEPTH
TAPS = 9 * CH
WIDE = 3 * CH
CHIPS = 4
CHUNKS = 9
BF = jnp.bfloat16
F32 = jnp.float32
MESH = pl.DeviceIdType.MESH


def matmul(left, right):
    return jnp.dot(left, right, preferred_element_type=F32)


def depth_of(shape, axis):
    return lax.broadcasted_iota(jnp.int32, shape, axis) % DEPTH


def combined(wide, step, mirrored):
    first, middle, last = (wide[:, i * CH : (i + 1) * CH] for i in range(3))
    if mirrored:
        first, last = last, first
    rows = wide.shape[0]
    depth = depth_of((rows, CH), 0)
    below = jnp.where(depth >= step, pltpu.roll(first, step, 0), 0.0)
    above = jnp.where(depth < DEPTH - step, pltpu.roll(last, rows - step, 0), 0.0)
    return middle + below + above


def store_transposed(target, slot, values, step):
    depth = depth_of((CH, CH), 1)
    for j in range(values.shape[0] // CH):
        block = jnp.transpose(values[j * CH : (j + 1) * CH, :])
        ahead = jnp.where(depth < DEPTH - step, pltpu.roll(block, CH - step, 1), 0.0)
        behind = jnp.where(depth >= step, pltpu.roll(block, step, 1), 0.0)
        columns = slice(j * CH, (j + 1) * CH)
        target[slot, 0:CH, columns] = ahead.astype(BF)
        target[slot, CH : 2 * CH, columns] = block.astype(BF)
        target[slot, 2 * CH : 3 * CH, columns] = behind.astype(BF)


def gates(values):
    sigma = 0.5 * jnp.tanh(0.5 * values) + 0.5
    return values * sigma, sigma * (1.0 + values * (1.0 - sigma))


def program(
    n_space,
    n_chan,
    feat,
    up,
    mask,
    w1f,
    w2f,
    w3f,
    w2b,
    w3b,
    coarse,
    out1,
    out2,
    out3,
    e1,
    e2,
    e3,
    e4,
    eu,
    d1,
    b2,
    v1f,
    v2f,
    v3f,
    v2b,
    v3b,
    st,
    gt,
    cf,
    part,
    cs,
    cr,
    zs,
    zr,
    xs,
    xr,
    ys,
    yr,
    fs,
    fr,
    send_sem,
    recv_sem,
    local_sem,
):
    space = lax.axis_index("space")
    chan = lax.axis_index("chan")
    core = lax.rem(space, 2)
    chip_x = lax.rem(lax.div(space, 2), CHIPS)
    chip_y = lax.div(space, 2 * CHIPS)

    def near(d_space, d_chan):
        return (
            lax.rem(space + (d_space + n_space), n_space),
            lax.rem(chan + (d_chan + n_chan), n_chan),
        )

    sibling = (space + 1 - 2 * core, chan)

    def x_peer(d):
        return (chip_y * (2 * CHIPS) + lax.rem(chip_x + d, CHIPS) * 2 + core, chan)

    def y_peer(d):
        return (lax.rem(chip_y + d, CHIPS) * (2 * CHIPS) + chip_x * 2 + core, chan)

    started = []

    def send(source, target, device):
        index = len(started)
        copy = pltpu.make_async_remote_copy(
            src_ref=source,
            dst_ref=target,
            send_sem=send_sem.at[index],
            recv_sem=recv_sem.at[index],
            device_id=device,
            device_id_type=MESH,
        )
        copy.start()
        started.append(copy)
        return copy

    local = []

    def fetch(source, target):
        copy = pltpu.make_async_copy(source, target, local_sem.at[len(local)])
        copy.start()
        local.append(copy)
        return copy

    peers = [near(a, b) for a in (-1, 0, 1) for b in (-1, 0, 1) if (a, b) != (0, 0)]
    peers.append(near(0, 2))
    peers += [x_peer(d) for d in range(1, CHIPS)]
    peers += [y_peer(d) for d in range(1, CHIPS)]
    barrier = pltpu.get_barrier_semaphore()
    for peer in peers:
        pl.semaphore_signal(barrier, inc=1, device_id=peer, device_id_type=MESH)
    get_e1 = fetch(feat, e1.at[pl.ds(1, ROWS), pl.ds(1, LENGTH)])
    get_eu = fetch(up, eu.at[pl.ds(0, 2), pl.ds(0, HALF)])
    get_v1f = fetch(w1f, v1f)
    get_v3b = fetch(w3b, v3b)
    get_v2f = fetch(w2f, v2f)
    get_v3f = fetch(w3f, v3f)
    get_v2b = fetch(w2b, v2b)
    pl.semaphore_wait(barrier, len(peers))

    in_x, in_y = pl.ds(1, ROWS), pl.ds(1, LENGTH)
    halo_one = [
        send(feat.at[ROWS - 1], e1.at[0, in_y], near(1, 0)),
        send(feat.at[0], e1.at[ROWS + 1, in_y], near(-1, 0)),
        send(feat.at[:, LENGTH - 1], e1.at[in_x, 0], near(0, 1)),
        send(feat.at[:, 0], e1.at[in_x, LENGTH + 1], near(0, -1)),
        send(feat.at[ROWS - 1, LENGTH - 1], e1.at[0, 0], near(1, 1)),
        send(feat.at[ROWS - 1, 0], e1.at[0, LENGTH + 1], near(1, -1)),
        send(feat.at[0, LENGTH - 1], e1.at[ROWS + 1, 0], near(-1, 1)),
        send(feat.at[0, 0], e1.at[ROWS + 1, LENGTH + 1], near(-1, -1)),
    ]
    halo_up = [
        send(up.at[0], eu.at[2, pl.ds(0, HALF)], near(-1, 0)),
        send(up.at[:, 0], eu.at[pl.ds(0, 2), HALF], near(0, -1)),
        send(up.at[0, 0], eu.at[2, HALF], near(-1, -1)),
    ]

    def arrived(copies):
        for copy in copies:
            copy.wait_recv()

    def clear(ref, width):
        rows, columns = ref.shape[0], ref.shape[1]

        @pl.when(space == 0)
        def _():
            ref[0:width] = jnp.zeros((width, columns, DEPTH, CH), BF)

        @pl.when(space == n_space - 1)
        def _():
            ref[rows - width : rows] = jnp.zeros((width, columns, DEPTH, CH), BF)

        @pl.when(chan == 0)
        def _():
            ref[:, 0:width] = jnp.zeros((rows, width, DEPTH, CH), BF)

        @pl.when(chan == n_chan - 1)
        def _():
            ref[:, columns - width : columns] = jnp.zeros((rows, width, DEPTH, CH), BF)

    def rim(ref, low):
        y = pl.ds(2, LENGTH)
        if low:
            near_rows, far_rows, to = pl.ds(2, 2), pl.ds(ROWS + 2, 2), -1
        else:
            near_rows, far_rows, to = pl.ds(ROWS, 2), pl.ds(0, 2), 1
        first, last = pl.ds(2, 2), pl.ds(LENGTH, 2)
        before, after = pl.ds(0, 2), pl.ds(LENGTH + 2, 2)
        return [
            send(ref.at[near_rows, y], ref.at[far_rows, y], near(to, 0)),
            send(ref.at[near_rows, last], ref.at[far_rows, before], near(to, 1)),
            send(ref.at[near_rows, first], ref.at[far_rows, after], near(to, -1)),
        ]

    def sides(ref):
        x = pl.ds(2, ROWS)
        return [
            send(ref.at[x, pl.ds(LENGTH, 2)], ref.at[x, pl.ds(0, 2)], near(0, 1)),
            send(ref.at[x, pl.ds(2, 2)], ref.at[x, pl.ds(LENGTH + 2, 2)], near(0, -1)),
        ]

    def flat(block):
        return block.reshape(-1, CH)

    def window(ref, x, begin, spread):
        return jnp.concatenate(
            [
                flat(ref[x + spread * ax, pl.ds(begin + spread * ay, HALF)])
                for ax in range(3)
                for ay in range(3)
            ],
            axis=1,
        )

    def fluid(half):
        cells = jnp.broadcast_to(mask[half][None], (HALF, DEPTH, CH))
        return flat(cells)

    def over(low, high, step):
        def one(i, carry):
            step(lax.div(i, 2), lax.rem(i, 2))
            return carry

        lax.fori_loop(low, high, one, 0)

    get_eu.wait()
    for qx in range(2):
        store_transposed(gt, qx, flat(eu[qx, 0:HALF]).astype(F32), 1)

    get_e1.wait()
    get_v1f.wait()
    arrived(halo_one)
    clear(e1, 1)

    def layer_one(x, half):
        pre = combined(matmul(window(e1, x, half * HALF, 1), v1f[...]), 1, False)
        hidden, slope = gates(pre)
        inside = fluid(half)
        block = (hidden * inside).astype(BF).reshape(HALF, DEPTH, CH)
        e2[2 + x, pl.ds(2 + half * HALF, HALF)] = block
        d1[x, half] = slope * inside

    over(0, 4, layer_one)
    halo_two = rim(e2, True)
    over(4, 8, layer_one)
    halo_two += rim(e2, False)
    halo_two += sides(e2)

    arrived(halo_up)
    get_v3b.wait()

    @pl.when(space == n_space - 1)
    def _():
        eu[2] = jnp.zeros((HALF + 1, DEPTH, CH), BF)

    @pl.when(chan == n_chan - 1)
    def _():
        eu[:, HALF] = jnp.zeros((3, DEPTH, CH), BF)

    routes = (((1, 0),), ((0, 1), (2, 0)))
    for qx in range(2):
        for px in range(2):
            for py in range(2):
                taps = [(ax, dx, ay, dy) for ax, dx in routes[px] for ay, dy in routes[py]]
                cells = [flat(eu[qx + dx, dy : dy + HALF]) for _, dx, _, dy in taps]
                rows = [v3b[(ax * 3 + ay) * CH : (ax * 3 + ay + 1) * CH, :] for ax, _, ay, _ in taps]
                if len(taps) > 1:
                    cells, rows = [jnp.concatenate(cells, axis=1)], [jnp.concatenate(rows, axis=0)]
                back = combined(matmul(cells[0], rows[0]), 1, True)
                b2[2 * qx + px, py] = back.astype(BF).reshape(HALF, DEPTH, CH)

    get_v2f.wait()
    arrived(halo_two)
    clear(e2, 2)

    def layer_two(x, half):
        pre = combined(matmul(window(e2, x, half * HALF, 2), v2f[...]), 2, False)
        hidden, slope = gates(pre)
        inside = fluid(half)
        pairs = (hidden * inside).astype(BF).reshape(HALF // 2, 2, DEPTH, CH)
        first = half * (HALF // 2)
        e3[1 + x, 1, pl.ds(first, HALF // 2)] = pairs[:, 0]
        e3[1 + x, 0, pl.ds(first + 1, HALF // 2)] = pairs[:, 1]
        back = [b2[x, r, pl.ds(first, HALF // 2)].astype(F32) for r in range(2)]
        back = flat(jnp.stack(back, axis=1))
        product = (back * inside * slope).astype(BF)
        e4[2 + x, pl.ds(2 + half * HALF, HALF)] = product.reshape(HALF, DEPTH, CH)
        store_transposed(st, 2 * x + half, product.astype(F32), 2)

    over(0, 4, layer_two)
    halo_four = rim(e4, True)
    over(4, 8, layer_two)
    halo_four += rim(e4, False)
    halo_four += sides(e4)
    evens, odds = pl.ds(0, HALF), pl.ds(1, HALF)
    halo_three = [
        send(e3.at[ROWS, 1, evens], e3.at[0, 1, evens], near(1, 0)),
        send(e3.at[ROWS, 0, odds], e3.at[0, 0, odds], near(1, 0)),
        send(e3.at[pl.ds(1, ROWS), 0, HALF], e3.at[pl.ds(1, ROWS), 0, 0], near(0, 1)),
        send(e3.at[ROWS, 0, HALF], e3.at[0, 0, 0], near(1, 1)),
    ]

    waits = {}

    def share_core(k):
        cs[k] = part[k, :, :, 1 - core].astype(BF)
        waits[k] = [send(cs.at[k], cr.at[k], sibling)]

    def share_chan(k):
        arrived(waits[k])
        waits[k] = []
        for d in range(1, n_chan):
            other = lax.rem(chan + d, n_chan)
            zs[k, d - 1] = (part[k, :, other, core] + cr[k, :, other].astype(F32)).astype(BF)
            waits[k].append(send(zs.at[k, d - 1], zr.at[k, d - 1], near(0, d)))

    def share_first(k):
        arrived(waits[k])
        total = part[k, :, chan, core] + cr[k, :, chan].astype(F32)
        for d in range(1, n_chan):
            total += zr[k, d - 1].astype(F32)
        xs[k] = total.astype(BF)
        peer = (x_peer, y_peer)[k % 2]
        waits[k] = [send(xs.at[k], xr.at[k, d - 1], peer(d)) for d in range(1, CHIPS)]

    def four(own, others, k):
        opposite = own[k].astype(F32) + others[k, 1].astype(F32)
        return opposite + (others[k, 0].astype(F32) + others[k, 2].astype(F32))

    def share_second(k):
        arrived(waits[k])
        ys[k] = four(xs, xr, k).astype(BF)
        peer = (y_peer, x_peer)[k % 2]
        waits[k] = [send(ys.at[k], yr.at[k, d - 1], peer(d)) for d in range(1, CHIPS)]

    def share_back(k):
        arrived(waits[k])
        total = four(ys, yr, k)
        fs[k] = jnp.concatenate([total[0], total[1], total[2]], axis=1)
        waits[k] = [send(fs.at[k], fr.at[k], sibling)]

    def finish(k):
        arrived(waits[k])
        out = (out2, out3, out1)[k // 3]
        columns = slice((k % 3) * TAPS, (k % 3 + 1) * TAPS)
        out[core, :, columns] = fs[k]
        out[1 - core, :, columns] = fr[k]

    stages = (share_core, share_chan, share_first, share_second, share_back, finish)
    progress = {}

    def advance(*chunks):
        for k in chunks:
            at = progress.get(k, 0)
            if at < len(stages):
                stages[at](k)
                progress[k] = at + 1

    def grads(k, ref, spread):
        ax = k % 3
        part[k] = jnp.zeros(part.shape[1:], F32)

        def one(x, carry):
            slopes = jnp.concatenate([st[2 * x], st[2 * x + 1]], axis=1)
            cells = [
                flat(ref[x + spread * ax, spread * ay : spread * ay + LENGTH]) for ay in range(3)
            ]
            product = matmul(slopes, jnp.concatenate(cells, axis=1))
            part[k] += product.reshape(part.shape[1:])
            return carry

        lax.fori_loop(0, ROWS, one, 0)

    def coarse_window(x):
        return [flat(e3[x, r, j : j + HALF]) for r, j in ((0, 0), (1, 0), (0, 1))]

    def coarse_grads(k):
        ax = k % 3
        total = 0.0
        for qx in range(2):
            cells = jnp.concatenate(coarse_window(2 * qx + ax), axis=1)
            total += matmul(gt[qx], cells)
        part[k] = total.reshape(part.shape[1:])

    for k in range(3):
        grads(k, e2, 2)
        advance(*range(k + 1))
    arrived(halo_three)
    get_v3f.wait()

    @pl.when(space == 0)
    def _():
        e3[0] = jnp.zeros(e3.shape[1:], BF)

    @pl.when(chan == 0)
    def _():
        e3[:, 0, 0] = jnp.zeros((ROWS + 1, DEPTH, CH), BF)

    for k in range(3, 6):
        coarse_grads(k)
        advance(*range(k + 1))
    for qx in range(2):
        cells = [block for ax in range(3) for block in coarse_window(2 * qx + ax)]
        cf[...] = combined(matmul(jnp.concatenate(cells, axis=1), v3f[...]), 1, False)
        for qz in range(DEPTH // 2):
            coarse[qx, qz] = cf[pl.ds(2 * qz, HALF, stride=DEPTH), :].astype(BF)
    advance(*range(6))
    get_v2b.wait()
    arrived(halo_four)
    clear(e4, 2)

    def layer_back(x, half):
        back = combined(matmul(mirror(x, half), v2b[...]), 2, True).astype(BF).astype(F32)
        slope = (back * d1[x, half]).astype(BF)
        store_transposed(st, 2 * x + half, slope.astype(F32), 1)

    def mirror(x, half):
        return jnp.concatenate(
            [
                flat(e4[x + 4 - 2 * ax, pl.ds(half * HALF + 4 - 2 * ay, HALF)])
                for ax in range(3)
                for ay in range(3)
            ],
            axis=1,
        )

    over(0, 4, layer_back)
    advance(*range(6))
    over(4, 8, layer_back)
    advance(*range(6))
    for k in range(6, 9):
        grads(k, e1, 1)
        advance(*range(k + 1))
    while any(progress[k] < len(stages) for k in range(CHUNKS)):
        advance(*range(CHUNKS))
    for copy in started:
        copy.wait_send()


def local(features, fluid_tiles, weight_one, weight_two, weight_three, upstream, sizes):
    n_space, n_chan = sizes
    feat = jnp.transpose(features, (0, 2, 1, 3))
    up = jnp.transpose(upstream, (0, 2, 1, 3))
    up = jnp.stack([up, jnp.zeros_like(up)], axis=3).reshape(2, HALF, DEPTH, CH)
    tiles = jnp.transpose(fluid_tiles[0], (1, 0)).astype(F32)
    mask = jnp.broadcast_to(jnp.repeat(tiles, TILE_Z, axis=1)[:, :, None], (2, DEPTH, CH))

    def forward(weight):
        return jnp.transpose(weight, (1, 3, 4, 2, 0)).reshape(TAPS, WIDE)

    def backward(weight):
        return jnp.transpose(weight, (1, 3, 0, 2, 4)).reshape(TAPS, WIDE)

    hbm = pl.BlockSpec(memory_space=pl.ANY)
    vmem = pl.BlockSpec(memory_space=pltpu.VMEM)
    grad_shape = jax.ShapeDtypeStruct((2, 16, 3 * TAPS), F32)
    copies = 31 + 11 * CHUNKS
    weight_shape = pltpu.VMEM((TAPS, WIDE), BF)
    piece = (CHUNKS, 3, 16, WIDE)
    pieces = (CHUNKS, 3, 3, 16, WIDE)
    coarse, grad_one, grad_two, grad_three = pl.pallas_call(
        functools.partial(program, n_space, n_chan),
        out_shape=(
            jax.ShapeDtypeStruct((2, DEPTH // 2, HALF, CH), BF),
            grad_shape,
            grad_shape,
            grad_shape,
        ),
        in_specs=[hbm, hbm, vmem, hbm, hbm, hbm, hbm, hbm],
        out_specs=[vmem] * 4,
        scratch_shapes=[
            pltpu.VMEM((ROWS + 2, LENGTH + 2, DEPTH, CH), BF),
            pltpu.VMEM((ROWS + 4, LENGTH + 4, DEPTH, CH), BF),
            pltpu.VMEM((ROWS + 1, 2, HALF + 1, DEPTH, CH), BF),
            pltpu.VMEM((ROWS + 4, LENGTH + 4, DEPTH, CH), BF),
            pltpu.VMEM((3, HALF + 1, DEPTH, CH), BF),
            pltpu.VMEM((ROWS, 2, CELLS, CH), F32),
            pltpu.VMEM((ROWS, 2, HALF, DEPTH, CH), BF),
            weight_shape,
            weight_shape,
            weight_shape,
            weight_shape,
            weight_shape,
            pltpu.VMEM((8, WIDE, CELLS), BF),
            pltpu.VMEM((2, WIDE, CELLS), BF),
            pltpu.VMEM((CELLS, CH), F32),
            pltpu.VMEM((CHUNKS, 3, n_chan, 2, 16, WIDE), F32),
            pltpu.VMEM((CHUNKS, 3, n_chan, 16, WIDE), BF),
            pltpu.VMEM((CHUNKS, 3, n_chan, 16, WIDE), BF),
            pltpu.VMEM(pieces, BF),
            pltpu.VMEM(pieces, BF),
            pltpu.VMEM(piece, BF),
            pltpu.VMEM(pieces, BF),
            pltpu.VMEM(piece, BF),
            pltpu.VMEM(pieces, BF),
            pltpu.VMEM((CHUNKS, 16, TAPS), F32),
            pltpu.VMEM((CHUNKS, 16, TAPS), F32),
            pltpu.SemaphoreType.DMA((copies,)),
            pltpu.SemaphoreType.DMA((copies,)),
            pltpu.SemaphoreType.DMA((7,)),
        ],
        compiler_params=pltpu.CompilerParams(
            collective_id=0, has_side_effects=True, vmem_limit_bytes=58 << 20
        ),
    )(
        feat,
        up,
        mask,
        forward(weight_one),
        forward(weight_two),
        forward(weight_three),
        backward(weight_two),
        backward(weight_three),
    )
    shape = (2 * 16, 3, 3, 3, CH)
    return (
        coarse,
        grad_one.reshape(shape),
        grad_two.reshape(shape),
        grad_three.reshape(shape),
    )


def solution(mesh):
    in_specs = (
        P("space", None, "chan", None),
        P("space", None, "chan"),
        P(),
        P(),
        P(),
        P("space", None, "chan", None),
    )
    out_specs = (
        P("space", None, "chan", None),
        P("chan", None, None, None, None),
        P("chan", None, None, None, None),
        P("chan", None, None, None, None),
    )
    sizes = (mesh.shape["space"], mesh.shape["chan"])
    return jax.shard_map(
        functools.partial(local, sizes=sizes),
        mesh=mesh,
        in_specs=in_specs,
        out_specs=out_specs,
        check_vma=False,
    )
```

```python
import functools

import jax
import jax.numpy as jnp
from jax import lax
from jax.experimental import pallas as pl
from jax.experimental.pallas import tpu as pltpu
from jax.sharding import PartitionSpec as P

TILE_Z = 4
TILE_Y = 32
ROWS = 4
LENGTH = 64
DEPTH = 16
CH = 128
HALF = LENGTH // 2
CELLS = HALF * DEPTH
TAPS = 9 * CH
WIDE = 3 * CH
CHIPS = 4
CHUNKS = 9
BF = jnp.bfloat16
F32 = jnp.float32
MESH = pl.DeviceIdType.MESH


def matmul_transposed(left, right):
    return lax.dot_general(left, right, (((1,), (1,)), ((), ())), preferred_element_type=F32)


def matmul(left, right):
    return jnp.dot(left, right, preferred_element_type=F32)


def depth_of(shape, axis):
    return lax.broadcasted_iota(jnp.int32, shape, axis) & (DEPTH - 1)


def rotated(values, step):
    turned = pltpu.roll(values.reshape(-1, 8, CH), step, 1)
    return turned.reshape(-1, 2, 8, CH)


def combined(wide, step, mirrored):
    first, middle, last = (wide[:, i * CH : (i + 1) * CH] for i in range(3))
    if mirrored:
        first, last = last, first
    depth = lax.broadcasted_iota(jnp.int32, (1, 8, CH), 1)
    low, high = depth < step, depth >= 8 - step
    down, up = rotated(first, step), rotated(last, 8 - step)
    upper = jnp.where(low, 0.0, down[:, 0]) + jnp.where(high, up[:, 1], up[:, 0])
    lower = jnp.where(low, down[:, 0], down[:, 1]) + jnp.where(high, 0.0, up[:, 1])
    return middle + jnp.stack([upper, lower], axis=1).reshape(-1, CH)


def store_transposed(target, slot, values, step):
    depth = depth_of((CH, CH), 1)
    for j in range(values.shape[0] // CH):
        block = jnp.transpose(values[j * CH : (j + 1) * CH, :])
        ahead = jnp.where(depth < DEPTH - step, pltpu.roll(block, CH - step, 1), 0.0)
        behind = jnp.where(depth >= step, pltpu.roll(block, step, 1), 0.0)
        columns = slice(j * CH, (j + 1) * CH)
        target[slot, 0:CH, columns] = ahead.astype(BF)
        target[slot, CH : 2 * CH, columns] = block.astype(BF)
        target[slot, 2 * CH : 3 * CH, columns] = behind.astype(BF)


def gates(values):
    sigma = 0.5 * jnp.tanh(0.5 * values) + 0.5
    return values * sigma, sigma * (1.0 + values * (1.0 - sigma))


def program(
    n_space,
    n_chan,
    feat,
    up,
    tiles,
    w1,
    w2,
    w3,
    coarse,
    out1,
    out2,
    out3,
    e1,
    e2,
    e3,
    e4,
    eu,
    d1,
    b2,
    v1f,
    v2f,
    v3f,
    v2b,
    v3b,
    st,
    gt,
    cf,
    raw_x,
    raw_up,
    wide,
    part,
    cs,
    cr,
    zs,
    zr,
    xs,
    xr,
    ys,
    yr,
    fs,
    fr,
    send_sem,
    recv_sem,
    local_sem,
):
    space = lax.axis_index("space")
    chan = lax.axis_index("chan")
    core = lax.rem(space, 2)
    chip_x = lax.rem(lax.div(space, 2), CHIPS)
    chip_y = lax.div(space, 2 * CHIPS)

    def near(d_space, d_chan):
        return (
            lax.rem(space + (d_space + n_space), n_space),
            lax.rem(chan + (d_chan + n_chan), n_chan),
        )

    sibling = (space + 1 - 2 * core, chan)

    def x_peer(d):
        return (chip_y * (2 * CHIPS) + lax.rem(chip_x + d, CHIPS) * 2 + core, chan)

    def y_peer(d):
        return (lax.rem(chip_y + d, CHIPS) * (2 * CHIPS) + chip_x * 2 + core, chan)

    started = []

    def send(source, target, device):
        index = len(started)
        copy = pltpu.make_async_remote_copy(
            src_ref=source,
            dst_ref=target,
            send_sem=send_sem.at[index],
            recv_sem=recv_sem.at[index],
            device_id=device,
            device_id_type=MESH,
        )
        copy.start()
        started.append(copy)
        return copy

    local = []

    def fetch(source, target):
        copy = pltpu.make_async_copy(source, target, local_sem.at[len(local)])
        copy.start()
        local.append(copy)
        return copy

    peers = [near(a, b) for a in (-1, 0, 1) for b in (-1, 0, 1) if (a, b) != (0, 0)]
    peers.append(near(0, 2))
    peers += [x_peer(d) for d in range(1, CHIPS)]
    peers += [y_peer(d) for d in range(1, CHIPS)]
    barrier = pltpu.get_barrier_semaphore()
    for peer in peers:
        pl.semaphore_signal(barrier, inc=1, device_id=peer, device_id_type=MESH)
    get_x = fetch(feat, raw_x)
    get_up = fetch(up, raw_up)

    def forward_weight(source, target):
        return [fetch(source.at[:, az], target.at[:, :, az]) for az in range(3)]

    def backward_weight(source, target):
        return [
            fetch(source.at[:, az], target.at[:, :, :, az * CH : (az + 1) * CH])
            for az in range(3)
        ]

    get_v1f = forward_weight(w1, v1f)
    get_v3b = backward_weight(w3, v3b)
    get_v2f = forward_weight(w2, v2f)
    get_v3f = forward_weight(w3, v3f)
    get_v2b = backward_weight(w2, v2b)

    def ready(copies):
        for copy in copies:
            copy.wait()

    get_x.wait()

    def turn(x, carry):
        for z in range(DEPTH):
            wide[pl.ds(z, LENGTH, stride=DEPTH), :] = raw_x[x, z].astype(F32)
        e1[1 + x, pl.ds(1, LENGTH)] = wide[...].astype(BF).reshape(LENGTH, DEPTH, CH)
        return carry

    lax.fori_loop(0, ROWS, turn, 0)
    get_up.wait()
    cf[...] = jnp.zeros_like(cf)
    for qx in range(2):
        for qz in range(DEPTH // 2):
            cf[pl.ds(2 * qz, HALF, stride=DEPTH), :] = raw_up[qx, qz].astype(F32)
        eu[qx, 0:HALF] = cf[...].astype(BF).reshape(HALF, DEPTH, CH)
    pl.semaphore_wait(barrier, len(peers))

    in_x, in_y = pl.ds(1, ROWS), pl.ds(1, LENGTH)
    top, right = ROWS, LENGTH
    halo_one = [
        send(e1.at[top, in_y], e1.at[0, in_y], near(1, 0)),
        send(e1.at[1, in_y], e1.at[top + 1, in_y], near(-1, 0)),
        send(e1.at[in_x, right], e1.at[in_x, 0], near(0, 1)),
        send(e1.at[in_x, 1], e1.at[in_x, right + 1], near(0, -1)),
        send(e1.at[top, right], e1.at[0, 0], near(1, 1)),
        send(e1.at[top, 1], e1.at[0, right + 1], near(1, -1)),
        send(e1.at[1, right], e1.at[top + 1, 0], near(-1, 1)),
        send(e1.at[1, 1], e1.at[top + 1, right + 1], near(-1, -1)),
    ]
    halo_up = [
        send(eu.at[0, pl.ds(0, HALF)], eu.at[2, pl.ds(0, HALF)], near(-1, 0)),
        send(eu.at[pl.ds(0, 2), 0], eu.at[pl.ds(0, 2), HALF], near(0, -1)),
        send(eu.at[0, 0], eu.at[2, HALF], near(-1, -1)),
    ]

    def arrived(copies):
        for copy in copies:
            copy.wait_recv()

    def clear(ref, width):
        rows, columns = ref.shape[0], ref.shape[1]

        @pl.when(space == 0)
        def _():
            ref[0:width] = jnp.zeros((width, columns, DEPTH, CH), BF)

        @pl.when(space == n_space - 1)
        def _():
            ref[rows - width : rows] = jnp.zeros((width, columns, DEPTH, CH), BF)

        @pl.when(chan == 0)
        def _():
            ref[:, 0:width] = jnp.zeros((rows, width, DEPTH, CH), BF)

        @pl.when(chan == n_chan - 1)
        def _():
            ref[:, columns - width : columns] = jnp.zeros((rows, width, DEPTH, CH), BF)

    def rim(ref, low):
        y = pl.ds(2, LENGTH)
        if low:
            near_rows, far_rows, to = pl.ds(2, 2), pl.ds(ROWS + 2, 2), -1
        else:
            near_rows, far_rows, to = pl.ds(ROWS, 2), pl.ds(0, 2), 1
        first, last = pl.ds(2, 2), pl.ds(LENGTH, 2)
        before, after = pl.ds(0, 2), pl.ds(LENGTH + 2, 2)
        return [
            send(ref.at[near_rows, y], ref.at[far_rows, y], near(to, 0)),
            send(ref.at[near_rows, last], ref.at[far_rows, before], near(to, 1)),
            send(ref.at[near_rows, first], ref.at[far_rows, after], near(to, -1)),
        ]

    def sides(ref):
        x = pl.ds(2, ROWS)
        return [
            send(ref.at[x, pl.ds(LENGTH, 2)], ref.at[x, pl.ds(0, 2)], near(0, 1)),
            send(ref.at[x, pl.ds(2, 2)], ref.at[x, pl.ds(LENGTH + 2, 2)], near(0, -1)),
        ]

    def flat(block):
        return block.reshape(-1, CH)

    def window(ref, x, begin, spread):
        return jnp.concatenate(
            [
                flat(ref[x + spread * ax, pl.ds(begin + spread * ay, HALF)])
                for ax in range(3)
                for ay in range(3)
            ],
            axis=1,
        )

    def fluid(half):
        depth = lax.broadcasted_iota(jnp.int32, (DEPTH, CH), 0)
        column = jnp.zeros((DEPTH, CH), jnp.int32)
        for i in range(DEPTH // TILE_Z):
            column = jnp.where(lax.div(depth, TILE_Z) == i, tiles[0, half, i], column)
        cells = jnp.broadcast_to(column.astype(F32)[None], (HALF, DEPTH, CH))
        return flat(cells)

    def taps_of(weight):
        blocks = [weight[ax, ay].reshape(WIDE, CH) for ax in range(3) for ay in range(3)]
        return jnp.concatenate(blocks, axis=1)

    def over(low, high, step):
        def one(i, carry):
            step(lax.div(i, 2), lax.rem(i, 2))
            return carry

        lax.fori_loop(low, high, one, 0)

    for qx in range(2):
        store_transposed(gt, qx, flat(eu[qx, 0:HALF]).astype(F32), 1)

    ready(get_v1f)
    arrived(halo_one)
    clear(e1, 1)

    def layer_one(x, half):
        pre = combined(matmul_transposed(window(e1, x, half * HALF, 1), taps_of(v1f)), 1, False)
        hidden, slope = gates(pre)
        inside = fluid(half)
        block = (hidden * inside).astype(BF).reshape(HALF, DEPTH, CH)
        e2[2 + x, pl.ds(2 + half * HALF, HALF)] = block
        d1[x, half] = slope * inside

    over(0, 4, layer_one)
    halo_two = rim(e2, True)
    over(4, 8, layer_one)
    halo_two += rim(e2, False)
    halo_two += sides(e2)

    arrived(halo_up)
    ready(get_v3b)

    @pl.when(space == n_space - 1)
    def _():
        eu[2] = jnp.zeros((HALF + 1, DEPTH, CH), BF)

    @pl.when(chan == n_chan - 1)
    def _():
        eu[:, HALF] = jnp.zeros((3, DEPTH, CH), BF)

    routes = (((1, 0),), ((0, 1), (2, 0)))
    for qx in range(2):
        for px in range(2):
            for py in range(2):
                taps = [(ax, dx, ay, dy) for ax, dx in routes[px] for ay, dy in routes[py]]
                cells = [flat(eu[qx + dx, dy : dy + HALF]) for _, dx, _, dy in taps]
                rows = [v3b[ax, ay] for ax, _, ay, _ in taps]
                if len(taps) > 1:
                    cells, rows = [jnp.concatenate(cells, axis=1)], [jnp.concatenate(rows, axis=0)]
                back = combined(matmul(cells[0], rows[0]), 1, True)
                b2[2 * qx + px, py] = back.astype(BF).reshape(HALF, DEPTH, CH)

    ready(get_v2f)
    arrived(halo_two)
    clear(e2, 2)

    def layer_two(x, half):
        pre = combined(matmul_transposed(window(e2, x, half * HALF, 2), taps_of(v2f)), 2, False)
        hidden, slope = gates(pre)
        inside = fluid(half)
        pairs = (hidden * inside).astype(BF).reshape(HALF // 2, 2, DEPTH, CH)
        first = half * (HALF // 2)
        e3[1 + x, 1, pl.ds(first, HALF // 2)] = pairs[:, 0]
        e3[1 + x, 0, pl.ds(first + 1, HALF // 2)] = pairs[:, 1]
        back = [b2[x, r, pl.ds(first, HALF // 2)].astype(F32) for r in range(2)]
        back = flat(jnp.stack(back, axis=1))
        product = (back * inside * slope).astype(BF)
        e4[2 + x, pl.ds(2 + half * HALF, HALF)] = product.reshape(HALF, DEPTH, CH)
        store_transposed(st, 2 * x + half, product.astype(F32), 2)

    over(0, 4, layer_two)
    halo_four = rim(e4, True)
    over(4, 8, layer_two)
    halo_four += rim(e4, False)
    halo_four += sides(e4)
    evens, odds = pl.ds(0, HALF), pl.ds(1, HALF)
    halo_three = [
        send(e3.at[ROWS, 1, evens], e3.at[0, 1, evens], near(1, 0)),
        send(e3.at[ROWS, 0, odds], e3.at[0, 0, odds], near(1, 0)),
        send(e3.at[pl.ds(1, ROWS), 0, HALF], e3.at[pl.ds(1, ROWS), 0, 0], near(0, 1)),
        send(e3.at[ROWS, 0, HALF], e3.at[0, 0, 0], near(1, 1)),
    ]

    waits = {}

    def share_core(k):
        cs[k] = part[k, :, :, 1 - core].astype(BF)
        waits[k] = [send(cs.at[k], cr.at[k], sibling)]

    def share_chan(k):
        arrived(waits[k])
        waits[k] = []
        for d in range(1, n_chan):
            other = lax.rem(chan + d, n_chan)
            zs[k, d - 1] = (part[k, :, other, core] + cr[k, :, other].astype(F32)).astype(BF)
            waits[k].append(send(zs.at[k, d - 1], zr.at[k, d - 1], near(0, d)))

    def share_first(k):
        arrived(waits[k])
        total = part[k, :, chan, core] + cr[k, :, chan].astype(F32)
        for d in range(1, n_chan):
            total += zr[k, d - 1].astype(F32)
        xs[k] = total.astype(BF)
        peer = (x_peer, y_peer)[k % 2]
        waits[k] = [send(xs.at[k], xr.at[k, d - 1], peer(d)) for d in range(1, CHIPS)]

    def four(own, others, k):
        opposite = own[k].astype(F32) + others[k, 1].astype(F32)
        return opposite + (others[k, 0].astype(F32) + others[k, 2].astype(F32))

    def share_second(k):
        arrived(waits[k])
        ys[k] = four(xs, xr, k).astype(BF)
        peer = (y_peer, x_peer)[k % 2]
        waits[k] = [send(ys.at[k], yr.at[k, d - 1], peer(d)) for d in range(1, CHIPS)]

    def share_back(k):
        arrived(waits[k])
        total = four(ys, yr, k)
        fs[k] = total
        waits[k] = [send(fs.at[k], fr.at[k], sibling)]

    def finish(k):
        arrived(waits[k])
        out = (out2, out3, out1)[k // 3]
        for ay in range(3):
            columns = slice(ay * CH, (ay + 1) * CH)
            out[k % 3, :, ay, core] = fs[k, :, :, columns]
            out[k % 3, :, ay, 1 - core] = fr[k, :, :, columns]

    stages = (share_core, share_chan, share_first, share_second, share_back, finish)
    progress = {}

    def advance(*chunks):
        for k in chunks:
            at = progress.get(k, 0)
            if at < len(stages):
                stages[at](k)
                progress[k] = at + 1

    def grads(k, ref, spread):
        ax = k % 3
        slopes = jnp.concatenate([st[i] for i in range(2 * ROWS)], axis=1)
        cells = jnp.concatenate(
            [
                jnp.concatenate(
                    [
                        flat(ref[x + spread * ax, spread * ay : spread * ay + LENGTH])
                        for ay in range(3)
                    ],
                    axis=1,
                )
                for x in range(ROWS)
            ],
            axis=0,
        )
        part[k] = matmul(slopes, cells).reshape(part.shape[1:])

    def coarse_window(x):
        return [flat(e3[x, r, j : j + HALF]) for r, j in ((0, 0), (1, 0), (0, 1))]

    def coarse_grads(k):
        ax = k % 3
        total = 0.0
        for qx in range(2):
            cells = jnp.concatenate(coarse_window(2 * qx + ax), axis=1)
            total += matmul(gt[qx], cells)
        part[k] = total.reshape(part.shape[1:])

    grads(0, e2, 2)
    advance(0)
    grads(1, e2, 2)
    advance(1, 0)
    grads(2, e2, 2)
    advance(2, 1, 0)
    arrived(halo_three)
    ready(get_v3f)

    @pl.when(space == 0)
    def _():
        e3[0] = jnp.zeros(e3.shape[1:], BF)

    @pl.when(chan == 0)
    def _():
        e3[:, 0, 0] = jnp.zeros((ROWS + 1, DEPTH, CH), BF)

    for k in range(3, 6):
        coarse_grads(k)
        advance(k)
    for qx in range(2):
        cells = [block for ax in range(3) for block in coarse_window(2 * qx + ax)]
        cf[...] = combined(matmul_transposed(jnp.concatenate(cells, axis=1), taps_of(v3f)), 1, False)
        for qz in range(DEPTH // 2):
            coarse[qx, qz] = cf[pl.ds(2 * qz, HALF, stride=DEPTH), :].astype(BF)
    advance(0, 1, 2)
    ready(get_v2b)
    arrived(halo_four)
    clear(e4, 2)

    def layer_back(x, half):
        back = combined(matmul(mirror(x, half), v2b[...].reshape(TAPS, WIDE)), 2, True).astype(BF).astype(F32)
        slope = (back * d1[x, half]).astype(BF)
        store_transposed(st, 2 * x + half, slope.astype(F32), 1)

    def mirror(x, half):
        return jnp.concatenate(
            [
                flat(e4[x + 4 - 2 * ax, pl.ds(half * HALF + 4 - 2 * ay, HALF)])
                for ax in range(3)
                for ay in range(3)
            ],
            axis=1,
        )

    over(0, 2, layer_back)
    advance(2, 3, 4, 5)
    over(2, 4, layer_back)
    advance(0, 1)
    over(4, 6, layer_back)
    advance(2, 3, 4, 5)
    over(6, 8, layer_back)
    advance(0, 1, 2)
    grads(6, e1, 1)
    advance(6, 3, 4, 5)
    grads(7, e1, 1)
    advance(7, 6, 1, 2)
    grads(8, e1, 1)
    advance(8, 7, 6, 3, 4, 5)
    while any(progress[k] < len(stages) for k in range(CHUNKS)):
        advance(*range(CHUNKS - 4, CHUNKS), *range(CHUNKS - 4))
    for copy in started:
        copy.wait_send()


def local(features, fluid_tiles, weight_one, weight_two, weight_three, upstream, sizes):
    n_space, n_chan = sizes
    tiles = jnp.transpose(fluid_tiles, (0, 2, 1))

    def by_tap(weight):
        return jnp.transpose(weight, (1, 2, 3, 0, 4))

    def by_output(grad):
        return jnp.transpose(grad.reshape(3, 3, 3, 2 * 16, CH), (3, 0, 1, 2, 4))

    hbm = pl.BlockSpec(memory_space=pl.ANY)
    vmem = pl.BlockSpec(memory_space=pltpu.VMEM)
    smem = pl.BlockSpec(memory_space=pltpu.SMEM)
    grad_shape = jax.ShapeDtypeStruct((3, 3, 3, 2, 16, CH), F32)
    copies = 31 + 11 * CHUNKS
    forward_shape = pltpu.VMEM((3, 3, 3, CH, CH), BF)
    backward_shape = pltpu.VMEM((3, 3, CH, WIDE), BF)
    piece = (CHUNKS, 3, 16, WIDE)
    pieces = (CHUNKS, 3, 3, 16, WIDE)
    coarse, grad_one, grad_two, grad_three = pl.pallas_call(
        functools.partial(program, n_space, n_chan),
        out_shape=(
            jax.ShapeDtypeStruct((2, DEPTH // 2, HALF, CH), BF),
            grad_shape,
            grad_shape,
            grad_shape,
        ),
        in_specs=[hbm, hbm, smem, hbm, hbm, hbm],
        out_specs=[vmem] * 4,
        scratch_shapes=[
            pltpu.VMEM((ROWS + 2, LENGTH + 2, DEPTH, CH), BF),
            pltpu.VMEM((ROWS + 4, LENGTH + 4, DEPTH, CH), BF),
            pltpu.VMEM((ROWS + 1, 2, HALF + 1, DEPTH, CH), BF),
            pltpu.VMEM((ROWS + 4, LENGTH + 4, DEPTH, CH), BF),
            pltpu.VMEM((3, HALF + 1, DEPTH, CH), BF),
            pltpu.VMEM((ROWS, 2, CELLS, CH), F32),
            pltpu.VMEM((ROWS, 2, HALF, DEPTH, CH), BF),
            forward_shape,
            forward_shape,
            forward_shape,
            backward_shape,
            backward_shape,
            pltpu.VMEM((8, WIDE, CELLS), BF),
            pltpu.VMEM((2, WIDE, CELLS), BF),
            pltpu.VMEM((CELLS, CH), F32),
            pltpu.VMEM((ROWS, DEPTH, LENGTH, CH), BF),
            pltpu.VMEM((2, DEPTH // 2, HALF, CH), BF),
            pltpu.VMEM((LENGTH * DEPTH, CH), F32),
            pltpu.VMEM((CHUNKS, 3, n_chan, 2, 16, WIDE), F32),
            pltpu.VMEM((CHUNKS, 3, n_chan, 16, WIDE), BF),
            pltpu.VMEM((CHUNKS, 3, n_chan, 16, WIDE), BF),
            pltpu.VMEM(pieces, BF),
            pltpu.VMEM(pieces, BF),
            pltpu.VMEM(piece, BF),
            pltpu.VMEM(pieces, BF),
            pltpu.VMEM(piece, BF),
            pltpu.VMEM(pieces, BF),
            pltpu.VMEM(piece, F32),
            pltpu.VMEM(piece, F32),
            pltpu.SemaphoreType.DMA((copies,)),
            pltpu.SemaphoreType.DMA((copies,)),
            pltpu.SemaphoreType.DMA((17,)),
        ],
        compiler_params=pltpu.CompilerParams(
            collective_id=0, has_side_effects=True, vmem_limit_bytes=58 << 20
        ),
    )(
        features,
        upstream,
        tiles,
        by_tap(weight_one),
        by_tap(weight_two),
        by_tap(weight_three),
    )
    return coarse, by_output(grad_one), by_output(grad_two), by_output(grad_three)


def solution(mesh):
    in_specs = (
        P("space", None, "chan", None),
        P("space", None, "chan"),
        P(),
        P(),
        P(),
        P("space", None, "chan", None),
    )
    out_specs = (
        P("space", None, "chan", None),
        P("chan", None, None, None, None),
        P("chan", None, None, None, None),
        P("chan", None, None, None, None),
    )
    sizes = (mesh.shape["space"], mesh.shape["chan"])
    return jax.shard_map(
        functools.partial(local, sizes=sizes),
        mesh=mesh,
        in_specs=in_specs,
        out_specs=out_specs,
        check_vma=False,
    )
```

```python
import functools

import jax
import jax.numpy as jnp
from jax import lax
from jax.experimental import pallas as pl
from jax.experimental.pallas import tpu as pltpu
from jax.sharding import PartitionSpec as P

TILE_Z = 4
TILE_Y = 32
ROWS = 4
LENGTH = 64
DEPTH = 16
CH = 128
HALF = LENGTH // 2
CELLS = HALF * DEPTH
TAPS = 9 * CH
WIDE = 3 * CH
CHIPS = 4
CHUNKS = 9
BF = jnp.bfloat16
F32 = jnp.float32
MESH = pl.DeviceIdType.MESH


def matmul_transposed(left, right):
    return lax.dot_general(left, right, (((1,), (1,)), ((), ())), preferred_element_type=F32)


def matmul(left, right):
    return jnp.dot(left, right, preferred_element_type=F32)


def depth_of(shape, axis):
    return lax.broadcasted_iota(jnp.int32, shape, axis) & (DEPTH - 1)


def rotated(values, step):
    turned = pltpu.roll(values.reshape(-1, 8, CH), step, 1)
    return turned.reshape(-1, 2, 8, CH)


def combined(wide, step, mirrored):
    first, middle, last = (wide[:, i * CH : (i + 1) * CH] for i in range(3))
    if mirrored:
        first, last = last, first
    depth = lax.broadcasted_iota(jnp.int32, (1, 8, CH), 1)
    low, high = depth < step, depth >= 8 - step
    down, up = rotated(first, step), rotated(last, 8 - step)
    upper = jnp.where(low, 0.0, down[:, 0]) + jnp.where(high, up[:, 1], up[:, 0])
    lower = jnp.where(low, down[:, 0], down[:, 1]) + jnp.where(high, 0.0, up[:, 1])
    return middle + jnp.stack([upper, lower], axis=1).reshape(-1, CH)


def store_transposed(target, slot, values, step):
    depth = depth_of((CH, CH), 1)
    for j in range(values.shape[0] // CH):
        block = jnp.transpose(values[j * CH : (j + 1) * CH, :])
        ahead = jnp.where(depth < DEPTH - step, pltpu.roll(block, CH - step, 1), 0.0)
        behind = jnp.where(depth >= step, pltpu.roll(block, step, 1), 0.0)
        columns = slice(j * CH, (j + 1) * CH)
        target[slot, 0:CH, columns] = ahead.astype(BF)
        target[slot, CH : 2 * CH, columns] = block.astype(BF)
        target[slot, 2 * CH : 3 * CH, columns] = behind.astype(BF)


def gates(values):
    sigma = 0.5 * jnp.tanh(0.5 * values) + 0.5
    return values * sigma, sigma * (1.0 + values * (1.0 - sigma))


def program(
    n_space,
    n_chan,
    feat,
    up,
    tiles,
    w1,
    w2,
    w3,
    coarse,
    out1,
    out2,
    out3,
    e1,
    e2,
    e3,
    e4,
    eu,
    d1,
    b2,
    v1f,
    v2f,
    v3f,
    v2b,
    v3b,
    st,
    gt,
    cf,
    raw_x,
    raw_up,
    wide,
    part,
    cs,
    cr,
    zs,
    zr,
    xs,
    xr,
    ys,
    yr,
    fs,
    fr,
    send_sem,
    recv_sem,
    local_sem,
):
    space = lax.axis_index("space")
    chan = lax.axis_index("chan")
    core = lax.rem(space, 2)
    chip_x = lax.rem(lax.div(space, 2), CHIPS)
    chip_y = lax.div(space, 2 * CHIPS)

    def near(d_space, d_chan):
        return (
            lax.rem(space + (d_space + n_space), n_space),
            lax.rem(chan + (d_chan + n_chan), n_chan),
        )

    sibling = (space + 1 - 2 * core, chan)

    def x_peer(d):
        return (chip_y * (2 * CHIPS) + lax.rem(chip_x + d, CHIPS) * 2 + core, chan)

    def y_peer(d):
        return (lax.rem(chip_y + d, CHIPS) * (2 * CHIPS) + chip_x * 2 + core, chan)

    started = []

    def send(source, target, device):
        index = len(started)
        copy = pltpu.make_async_remote_copy(
            src_ref=source,
            dst_ref=target,
            send_sem=send_sem.at[index],
            recv_sem=recv_sem.at[index],
            device_id=device,
            device_id_type=MESH,
        )
        copy.start()
        started.append(copy)
        return copy

    local = []

    def fetch(source, target):
        copy = pltpu.make_async_copy(source, target, local_sem.at[len(local)])
        copy.start()
        local.append(copy)
        return copy

    peers = [near(a, b) for a in (-1, 0, 1) for b in (-1, 0, 1) if (a, b) != (0, 0)]
    peers.append(near(0, 2))
    peers += [x_peer(d) for d in range(1, CHIPS)]
    peers += [y_peer(d) for d in range(1, CHIPS)]
    barrier = pltpu.get_barrier_semaphore()
    for peer in peers:
        pl.semaphore_signal(barrier, inc=1, device_id=peer, device_id_type=MESH)
    get_x = fetch(feat, raw_x)
    get_up = fetch(up, raw_up)

    def forward_weight(source, target):
        return [fetch(source.at[:, az], target.at[:, :, az]) for az in range(3)]

    def backward_weight(source, target):
        return [
            fetch(source.at[:, az], target.at[:, :, :, az * CH : (az + 1) * CH])
            for az in range(3)
        ]

    get_v1f = forward_weight(w1, v1f)
    get_v3b = backward_weight(w3, v3b)
    get_v2f = forward_weight(w2, v2f)
    get_v3f = forward_weight(w3, v3f)
    get_v2b = backward_weight(w2, v2b)

    def ready(copies):
        for copy in copies:
            copy.wait()

    get_x.wait()

    def turn(x, carry):
        for z in range(DEPTH):
            wide[pl.ds(z, LENGTH, stride=DEPTH), :] = raw_x[x, z].astype(F32)
        e1[1 + x, pl.ds(1, LENGTH)] = wide[...].astype(BF).reshape(LENGTH, DEPTH, CH)
        return carry

    lax.fori_loop(0, ROWS, turn, 0)
    get_up.wait()
    cf[...] = jnp.zeros_like(cf)
    for qx in range(2):
        for qz in range(DEPTH // 2):
            cf[pl.ds(2 * qz, HALF, stride=DEPTH), :] = raw_up[qx, qz].astype(F32)
        eu[qx, 0:HALF] = cf[...].astype(BF).reshape(HALF, DEPTH, CH)
    pl.semaphore_wait(barrier, len(peers))

    in_x, in_y = pl.ds(1, ROWS), pl.ds(1, LENGTH)
    top, right = ROWS, LENGTH
    sides = [
        send(e1.at[in_x, right], e1.at[in_x, 0], near(0, 1)),
        send(e1.at[in_x, 1], e1.at[in_x, right + 1], near(0, -1)),
    ]
    below = [
        send(e1.at[top, right], e1.at[0, 0], near(1, 1)),
        send(e1.at[top, 1], e1.at[0, right + 1], near(1, -1)),
        send(e1.at[top, in_y], e1.at[0, in_y], near(1, 0)),
    ]
    above = [
        send(e1.at[1, right], e1.at[top + 1, 0], near(-1, 1)),
        send(e1.at[1, 1], e1.at[top + 1, right + 1], near(-1, -1)),
        send(e1.at[1, in_y], e1.at[top + 1, in_y], near(-1, 0)),
    ]
    due_one = {0: below, 1: sides, 2: [], 3: [], 4: [], top + 1: above}
    halo_up = [
        send(eu.at[0, pl.ds(0, HALF)], eu.at[2, pl.ds(0, HALF)], near(-1, 0)),
        send(eu.at[pl.ds(0, 2), 0], eu.at[pl.ds(0, 2), HALF], near(0, -1)),
        send(eu.at[0, 0], eu.at[2, HALF], near(-1, -1)),
    ]

    def arrived(copies):
        for copy in copies:
            copy.wait_recv()

    def clear(ref, row, width):
        rows, columns = ref.shape[0], ref.shape[1]
        line = jnp.zeros((columns, DEPTH, CH), BF)
        corner = jnp.zeros((width, DEPTH, CH), BF)
        if row < width:

            @pl.when(space == 0)
            def _():
                ref[row] = line

        if row >= rows - width:

            @pl.when(space == n_space - 1)
            def _():
                ref[row] = line

        @pl.when(chan == 0)
        def _():
            ref[row, 0:width] = corner

        @pl.when(chan == n_chan - 1)
        def _():
            ref[row, columns - width : columns] = corner

    def need(ref, due, width, *rows):
        for row in rows:
            if row in due:
                arrived(due.pop(row))
                clear(ref, row, width)

    def spread_row(ref, due, x):
        own = x + 2
        far, to = (own + ROWS, -1) if x < 2 else (own - ROWS, 1)
        first, last, y = pl.ds(2, 2), pl.ds(LENGTH, 2), pl.ds(2, LENGTH)
        before, after = pl.ds(0, 2), pl.ds(LENGTH + 2, 2)
        due[own] = [
            send(ref.at[own, last], ref.at[own, before], near(0, 1)),
            send(ref.at[own, first], ref.at[own, after], near(0, -1)),
        ]
        due[far] = [
            send(ref.at[own, last], ref.at[far, before], near(to, 1)),
            send(ref.at[own, first], ref.at[far, after], near(to, -1)),
            send(ref.at[own, y], ref.at[far, y], near(to, 0)),
        ]

    def flat(block):
        return block.reshape(-1, CH)

    def window(ref, x, begin, spread):
        return jnp.concatenate(
            [
                flat(ref[x + spread * ax, pl.ds(begin + spread * ay, HALF)])
                for ax in range(3)
                for ay in range(3)
            ],
            axis=1,
        )

    def fluid(half):
        depth = lax.broadcasted_iota(jnp.int32, (DEPTH, CH), 0)
        column = jnp.zeros((DEPTH, CH), jnp.int32)
        for i in range(DEPTH // TILE_Z):
            column = jnp.where(lax.div(depth, TILE_Z) == i, tiles[0, half, i], column)
        cells = jnp.broadcast_to(column.astype(F32)[None], (HALF, DEPTH, CH))
        return flat(cells)

    def taps_of(weight):
        blocks = [weight[ax, ay].reshape(WIDE, CH) for ax in range(3) for ay in range(3)]
        return jnp.concatenate(blocks, axis=1)

    def over(low, high, step):
        def one(i, carry):
            step(lax.div(i, 2), lax.rem(i, 2))
            return carry

        lax.fori_loop(low, high, one, 0)

    for qx in range(2):
        store_transposed(gt, qx, flat(eu[qx, 0:HALF]).astype(F32), 1)

    ready(get_v1f)

    def layer_one(x, half):
        pre = combined(matmul_transposed(window(e1, x, half * HALF, 1), taps_of(v1f)), 1, False)
        hidden, slope = gates(pre)
        inside = fluid(half)
        block = (hidden * inside).astype(BF).reshape(HALF, DEPTH, CH)
        e2[2 + x, pl.ds(2 + half * HALF, HALF)] = block
        d1[x, half] = slope * inside

    due_two, due_four = {}, {}
    need(e1, due_one, 1, 1, 2, 3, 4)
    over(2, 6, layer_one)
    spread_row(e2, due_two, 1)
    spread_row(e2, due_two, 2)
    need(e1, due_one, 1, 0)
    over(0, 2, layer_one)
    spread_row(e2, due_two, 0)
    need(e1, due_one, 1, top + 1)
    over(6, 8, layer_one)
    spread_row(e2, due_two, 3)

    arrived(halo_up)
    ready(get_v3b)

    @pl.when(space == n_space - 1)
    def _():
        eu[2] = jnp.zeros((HALF + 1, DEPTH, CH), BF)

    @pl.when(chan == n_chan - 1)
    def _():
        eu[:, HALF] = jnp.zeros((3, DEPTH, CH), BF)

    routes = (((1, 0),), ((0, 1), (2, 0)))
    for qx in range(2):
        for px in range(2):
            for py in range(2):
                taps = [(ax, dx, ay, dy) for ax, dx in routes[px] for ay, dy in routes[py]]
                cells = [flat(eu[qx + dx, dy : dy + HALF]) for _, dx, _, dy in taps]
                rows = [v3b[ax, ay] for ax, _, ay, _ in taps]
                if len(taps) > 1:
                    cells, rows = [jnp.concatenate(cells, axis=1)], [jnp.concatenate(rows, axis=0)]
                back = combined(matmul(cells[0], rows[0]), 1, True)
                b2[2 * qx + px, py] = back.astype(BF).reshape(HALF, DEPTH, CH)

    ready(get_v2f)

    def layer_two(x, half):
        pre = combined(matmul_transposed(window(e2, x, half * HALF, 2), taps_of(v2f)), 2, False)
        hidden, slope = gates(pre)
        inside = fluid(half)
        pairs = (hidden * inside).astype(BF).reshape(HALF // 2, 2, DEPTH, CH)
        first = half * (HALF // 2)
        e3[1 + x, 1, pl.ds(first, HALF // 2)] = pairs[:, 0]
        e3[1 + x, 0, pl.ds(first + 1, HALF // 2)] = pairs[:, 1]
        back = [b2[x, r, pl.ds(first, HALF // 2)].astype(F32) for r in range(2)]
        back = flat(jnp.stack(back, axis=1))
        product = (back * inside * slope).astype(BF)
        e4[2 + x, pl.ds(2 + half * HALF, HALF)] = product.reshape(HALF, DEPTH, CH)
        store_transposed(st, 2 * x + half, product.astype(F32), 2)

    evens, odds = pl.ds(0, HALF), pl.ds(1, HALF)
    inner = pl.ds(1, ROWS)
    halo_three = []
    for x in (3, 2, 1, 0):
        need(e2, due_two, 2, x, x + 2, x + 4)
        over(2 * x, 2 * x + 2, layer_two)
        spread_row(e4, due_four, x)
        if x == 3:
            halo_three += [
                send(e3.at[ROWS, 0, HALF], e3.at[0, 0, 0], near(1, 1)),
                send(e3.at[ROWS, 1, evens], e3.at[0, 1, evens], near(1, 0)),
                send(e3.at[ROWS, 0, odds], e3.at[0, 0, odds], near(1, 0)),
            ]
    halo_three.append(send(e3.at[inner, 0, HALF], e3.at[inner, 0, 0], near(0, 1)))

    waits = {}

    def place(k):
        if k < CHUNKS - 1:
            return k, slice(None)
        j = k - (CHUNKS - 1)
        return CHUNKS - 1, slice(j * CH, (j + 1) * CH)

    def share_core(k):
        b, w = place(k)
        cs[b, :, :, :, w] = part[b, :, :, 1 - core, :, w].astype(BF)
        waits[k] = [send(cs.at[b, :, :, :, w], cr.at[b, :, :, :, w], sibling)]

    def share_chan(k):
        b, w = place(k)
        arrived(waits[k])
        waits[k] = []
        for d in (2, 1, 3)[: n_chan - 1]:
            other = lax.rem(chan + d, n_chan)
            total = part[b, :, other, core, :, w] + cr[b, :, other, :, w].astype(F32)
            zs[b, d - 1, :, :, w] = total.astype(BF)
            block = (b, d - 1, slice(None), slice(None), w)
            waits[k].append(send(zs.at[block], zr.at[block], near(0, d)))

    def scatter(k, source, target, peer):
        b, w = place(k)
        waits[k] = [
            send(source.at[b, :, :, w], target.at[b, d - 1, :, :, w], peer(d)) for d in (2, 1, 3)
        ]

    def share_first(k):
        b, w = place(k)
        arrived(waits[k])
        total = part[b, :, chan, core, :, w] + cr[b, :, chan, :, w].astype(F32)
        for d in range(1, n_chan):
            total += zr[b, d - 1, :, :, w].astype(F32)
        xs[b, :, :, w] = total.astype(BF)
        scatter(k, xs, xr, (x_peer, y_peer)[k % 2])

    def four(own, others, k):
        b, w = place(k)
        opposite = own[b, :, :, w].astype(F32) + others[b, 1, :, :, w].astype(F32)
        return opposite + (others[b, 0, :, :, w].astype(F32) + others[b, 2, :, :, w].astype(F32))

    def share_second(k):
        b, w = place(k)
        arrived(waits[k])
        ys[b, :, :, w] = four(xs, xr, k).astype(BF)
        scatter(k, ys, yr, (y_peer, x_peer)[k % 2])

    def share_back(k):
        b, w = place(k)
        arrived(waits[k])
        fs[b, :, :, w] = four(ys, yr, k)
        waits[k] = [send(fs.at[b, :, :, w], fr.at[b, :, :, w], sibling)]

    def finish(k):
        b, _ = place(k)
        arrived(waits[k])
        out = (out2, out3, out1)[b // 3]
        for ay in range(3) if b == k and k < CHUNKS - 1 else (k - CHUNKS + 1,):
            columns = slice(ay * CH, (ay + 1) * CH)
            out[b % 3, :, ay, core] = fs[b, :, :, columns]
            out[b % 3, :, ay, 1 - core] = fr[b, :, :, columns]

    stages = (share_core, share_chan, share_first, share_second, share_back, finish)
    progress = {}

    def advance(*chunks):
        for k in chunks:
            at = progress.get(k, 0)
            if at < len(stages):
                stages[at](k)
                progress[k] = at + 1

    def grads(k, ref, spread):
        ax = k % 3
        slopes = jnp.concatenate([st[i] for i in range(2 * ROWS)], axis=1)
        cells = jnp.concatenate(
            [
                jnp.concatenate(
                    [
                        flat(ref[x + spread * ax, spread * ay : spread * ay + LENGTH])
                        for ay in range(3)
                    ],
                    axis=1,
                )
                for x in range(ROWS)
            ],
            axis=0,
        )
        part[k] = matmul(slopes, cells).reshape(part.shape[1:])

    def coarse_window(x):
        return [flat(e3[x, r, j : j + HALF]) for r, j in ((0, 0), (1, 0), (0, 1))]

    def coarse_grads(k):
        ax = k % 3
        total = 0.0
        for qx in range(2):
            cells = jnp.concatenate(coarse_window(2 * qx + ax), axis=1)
            total += matmul(gt[qx], cells)
        part[k] = total.reshape(part.shape[1:])

    grads(0, e2, 2)
    advance(0)
    grads(1, e2, 2)
    advance(1)
    grads(2, e2, 2)
    advance(2, 0)
    arrived(halo_three)
    ready(get_v3f)

    @pl.when(space == 0)
    def _():
        e3[0] = jnp.zeros(e3.shape[1:], BF)

    @pl.when(chan == 0)
    def _():
        e3[:, 0, 0] = jnp.zeros((ROWS + 1, DEPTH, CH), BF)

    for k in range(3, 6):
        coarse_grads(k)
        advance(k)

    def coarse_rows(qx):
        cells = [block for ax in range(3) for block in coarse_window(2 * qx + ax)]
        cells = jnp.concatenate(cells, axis=1)
        cf[...] = combined(matmul_transposed(cells, taps_of(v3f)), 1, False)
        for qz in range(DEPTH // 2):
            coarse[qx, qz] = cf[pl.ds(2 * qz, HALF, stride=DEPTH), :].astype(BF)

    advance(1)
    ready(get_v2b)

    def layer_back(x, half):
        back = combined(matmul(mirror(x, half), v2b[...].reshape(TAPS, WIDE)), 2, True).astype(BF).astype(F32)
        slope = (back * d1[x, half]).astype(BF)
        store_transposed(st, 2 * x + half, slope.astype(F32), 1)

    def mirror(x, half):
        return jnp.concatenate(
            [
                flat(e4[x + 4 - 2 * ax, pl.ds(half * HALF + 4 - 2 * ay, HALF)])
                for ax in range(3)
                for ay in range(3)
            ],
            axis=1,
        )

    for x in (1, 0, 3, 2):
        need(e4, due_four, 2, x, x + 2, x + 4)
        over(2 * x, 2 * x + 2, layer_back)
        advance(*((2, 0) if x in (1, 3) else (3, 4, 5, 1)))
    grads(6, e1, 1)
    advance(6, 2, 0)
    grads(7, e1, 1)
    advance(7, 3, 4, 5)
    grads(8, e1, 1)
    advance(8, 9, 10, 6, 1)
    coarse_rows(0)
    advance(7, 0, 2)
    coarse_rows(1)
    advance(8, 9, 10, 3, 4, 5, 6, 1, 7, 2)
    last = (6, 7, 8, 9, 10)
    advance(8, 9, 10, 6, 3, 4, 5, 7)
    while any(progress[k] < len(stages) for k in last):
        advance(*last)
    for copy in started:
        copy.wait_send()


def write_out(*refs):
    count = len(refs) // 2
    sources, targets, sems = refs[:count], refs[count:-1], refs[-1]
    copies = [
        pltpu.make_async_copy(a, b, sems.at[i]) for i, (a, b) in enumerate(zip(sources, targets))
    ]
    for copy in copies:
        copy.start()
    for copy in copies:
        copy.wait()


def local(features, fluid_tiles, weight_one, weight_two, weight_three, upstream, sizes):
    n_space, n_chan = sizes
    tiles = jnp.transpose(fluid_tiles, (0, 2, 1))

    def by_tap(weight):
        return jnp.transpose(weight, (1, 2, 3, 0, 4))

    def by_output(grad):
        return jnp.transpose(grad.reshape(3, 3, 3, 2 * 16, CH), (3, 0, 1, 2, 4))

    hbm = pl.BlockSpec(memory_space=pl.ANY)
    vmem = pl.BlockSpec(memory_space=pltpu.VMEM)
    smem = pl.BlockSpec(memory_space=pltpu.SMEM)
    grad_shape = jax.ShapeDtypeStruct((3, 3, 3, 2, 16, CH), F32)
    copies = 55 + 11 * (CHUNKS + 2)
    forward_shape = pltpu.VMEM((3, 3, 3, CH, CH), BF)
    backward_shape = pltpu.VMEM((3, 3, CH, WIDE), BF)
    piece = (CHUNKS, 3, 16, WIDE)
    pieces = (CHUNKS, 3, 3, 16, WIDE)
    results = pl.pallas_call(
        functools.partial(program, n_space, n_chan),
        out_shape=(
            jax.ShapeDtypeStruct((2, DEPTH // 2, HALF, CH), BF),
            grad_shape,
            grad_shape,
            grad_shape,
        ),
        in_specs=[hbm, hbm, smem, hbm, hbm, hbm],
        out_specs=[vmem] * 4,
        scratch_shapes=[
            pltpu.VMEM((ROWS + 2, LENGTH + 2, DEPTH, CH), BF),
            pltpu.VMEM((ROWS + 4, LENGTH + 4, DEPTH, CH), BF),
            pltpu.VMEM((ROWS + 1, 2, HALF + 1, DEPTH, CH), BF),
            pltpu.VMEM((ROWS + 4, LENGTH + 4, DEPTH, CH), BF),
            pltpu.VMEM((3, HALF + 1, DEPTH, CH), BF),
            pltpu.VMEM((ROWS, 2, CELLS, CH), F32),
            pltpu.VMEM((ROWS, 2, HALF, DEPTH, CH), BF),
            forward_shape,
            forward_shape,
            forward_shape,
            backward_shape,
            backward_shape,
            pltpu.VMEM((8, WIDE, CELLS), BF),
            pltpu.VMEM((2, WIDE, CELLS), BF),
            pltpu.VMEM((CELLS, CH), F32),
            pltpu.VMEM((ROWS, DEPTH, LENGTH, CH), BF),
            pltpu.VMEM((2, DEPTH // 2, HALF, CH), BF),
            pltpu.VMEM((LENGTH * DEPTH, CH), F32),
            pltpu.VMEM((CHUNKS, 3, n_chan, 2, 16, WIDE), F32),
            pltpu.VMEM((CHUNKS, 3, n_chan, 16, WIDE), BF),
            pltpu.VMEM((CHUNKS, 3, n_chan, 16, WIDE), BF),
            pltpu.VMEM(pieces, BF),
            pltpu.VMEM(pieces, BF),
            pltpu.VMEM(piece, BF),
            pltpu.VMEM(pieces, BF),
            pltpu.VMEM(piece, BF),
            pltpu.VMEM(pieces, BF),
            pltpu.VMEM(piece, F32),
            pltpu.VMEM(piece, F32),
            pltpu.SemaphoreType.DMA((copies,)),
            pltpu.SemaphoreType.DMA((copies,)),
            pltpu.SemaphoreType.DMA((17,)),
        ],
        compiler_params=pltpu.CompilerParams(
            collective_id=0, has_side_effects=True, vmem_limit_bytes=58 << 20
        ),
    )(
        features,
        upstream,
        tiles,
        by_tap(weight_one),
        by_tap(weight_two),
        by_tap(weight_three),
    )
    coarse, grad_one, grad_two, grad_three = pl.pallas_call(
        write_out,
        out_shape=tuple(jax.ShapeDtypeStruct(r.shape, r.dtype) for r in results),
        in_specs=[hbm] * 4,
        out_specs=[hbm] * 4,
        scratch_shapes=[pltpu.SemaphoreType.DMA((4,))],
    )(*results)
    return coarse, by_output(grad_one), by_output(grad_two), by_output(grad_three)


def solution(mesh):
    in_specs = (
        P("space", None, "chan", None),
        P("space", None, "chan"),
        P(),
        P(),
        P(),
        P("space", None, "chan", None),
    )
    out_specs = (
        P("space", None, "chan", None),
        P("chan", None, None, None, None),
        P("chan", None, None, None, None),
        P("chan", None, None, None, None),
    )
    sizes = (mesh.shape["space"], mesh.shape["chan"])
    return jax.shard_map(
        functools.partial(local, sizes=sizes),
        mesh=mesh,
        in_specs=in_specs,
        out_specs=out_specs,
        check_vma=False,
    )
```

```python
import functools

import jax
import jax.numpy as jnp
from jax import lax
from jax.experimental import pallas as pl
from jax.experimental.pallas import tpu as pltpu
from jax.sharding import PartitionSpec as P

TILE_Z = 4
TILE_Y = 32
ROWS = 4
LENGTH = 64
DEPTH = 16
CH = 128
HALF = LENGTH // 2
CELLS = HALF * DEPTH
TAPS = 9 * CH
WIDE = 3 * CH
CHIPS = 4
CHUNKS = 9
BF = jnp.bfloat16
F32 = jnp.float32
MESH = pl.DeviceIdType.MESH


def matmul_transposed(left, right):
    return lax.dot_general(left, right, (((1,), (1,)), ((), ())), preferred_element_type=F32)


def matmul(left, right):
    return jnp.dot(left, right, preferred_element_type=F32)


def depth_of(shape, axis):
    return lax.broadcasted_iota(jnp.int32, shape, axis) & (DEPTH - 1)


def rotated(values, step):
    turned = pltpu.roll(values.reshape(-1, 8, CH), step, 1)
    return turned.reshape(-1, 2, 8, CH)


def combined(wide, step, mirrored):
    first, middle, last = (wide[:, i * CH : (i + 1) * CH] for i in range(3))
    if mirrored:
        first, last = last, first
    depth = lax.broadcasted_iota(jnp.int32, (1, 8, CH), 1)
    low, high = depth < step, depth >= 8 - step
    down, up = rotated(first, step), rotated(last, 8 - step)
    upper = jnp.where(low, 0.0, down[:, 0]) + jnp.where(high, up[:, 1], up[:, 0])
    lower = jnp.where(low, down[:, 0], down[:, 1]) + jnp.where(high, 0.0, up[:, 1])
    return middle + jnp.stack([upper, lower], axis=1).reshape(-1, CH)


def store_transposed(target, slot, values, step):
    depth = depth_of((CH, CH), 1)
    for j in range(values.shape[0] // CH):
        block = jnp.transpose(values[j * CH : (j + 1) * CH, :])
        ahead = jnp.where(depth < DEPTH - step, pltpu.roll(block, CH - step, 1), 0.0)
        behind = jnp.where(depth >= step, pltpu.roll(block, step, 1), 0.0)
        columns = slice(j * CH, (j + 1) * CH)
        target[slot, 0:CH, columns] = ahead.astype(BF)
        target[slot, CH : 2 * CH, columns] = block.astype(BF)
        target[slot, 2 * CH : 3 * CH, columns] = behind.astype(BF)


def gates(values):
    sigma = 0.5 * jnp.tanh(0.5 * values) + 0.5
    return values * sigma, sigma * (1.0 + values * (1.0 - sigma))


def program(
    n_space,
    n_chan,
    feat,
    up,
    tiles,
    w1,
    w2,
    w3,
    coarse,
    out1,
    out2,
    out3,
    e1,
    e2,
    e3,
    e4,
    eu,
    d1,
    b2,
    v1f,
    v2f,
    v3f,
    v2b,
    v3b,
    st,
    gt,
    cf,
    raw_x,
    raw_up,
    wide,
    part,
    cs,
    cr,
    zs,
    zr,
    xs,
    xr,
    ys,
    yr,
    fs,
    fr,
    send_sem,
    recv_sem,
    local_sem,
):
    space = lax.axis_index("space")
    chan = lax.axis_index("chan")
    core = lax.rem(space, 2)
    chip_x = lax.rem(lax.div(space, 2), CHIPS)
    chip_y = lax.div(space, 2 * CHIPS)

    def near(d_space, d_chan):
        return (
            lax.rem(space + (d_space + n_space), n_space),
            lax.rem(chan + (d_chan + n_chan), n_chan),
        )

    sibling = (space + 1 - 2 * core, chan)

    def x_peer(d):
        return (chip_y * (2 * CHIPS) + lax.rem(chip_x + d, CHIPS) * 2 + core, chan)

    def y_peer(d):
        return (lax.rem(chip_y + d, CHIPS) * (2 * CHIPS) + chip_x * 2 + core, chan)

    started = []

    def send(source, target, device):
        index = len(started)
        copy = pltpu.make_async_remote_copy(
            src_ref=source,
            dst_ref=target,
            send_sem=send_sem.at[index],
            recv_sem=recv_sem.at[index],
            device_id=device,
            device_id_type=MESH,
        )
        copy.start()
        started.append(copy)
        return copy

    local = []

    def fetch(source, target):
        copy = pltpu.make_async_copy(source, target, local_sem.at[len(local)])
        copy.start()
        local.append(copy)
        return copy

    peers = [near(a, b) for a in (-1, 0, 1) for b in (-1, 0, 1) if (a, b) != (0, 0)]
    peers.append(near(0, 2))
    peers += [x_peer(d) for d in range(1, CHIPS)]
    peers += [y_peer(d) for d in range(1, CHIPS)]
    barrier = pltpu.get_barrier_semaphore()
    for peer in peers:
        pl.semaphore_signal(barrier, inc=1, device_id=peer, device_id_type=MESH)
    get_x = fetch(feat, raw_x)
    get_up = fetch(up, raw_up)

    def forward_weight(source, target):
        return [fetch(source.at[:, az], target.at[:, :, az]) for az in range(3)]

    def backward_weight(source, target):
        return [
            fetch(source.at[:, az], target.at[:, :, :, az * CH : (az + 1) * CH])
            for az in range(3)
        ]

    get_v1f = forward_weight(w1, v1f)
    get_v3b = backward_weight(w3, v3b)
    get_v2f = forward_weight(w2, v2f)
    get_v3f = forward_weight(w3, v3f)
    get_v2b = backward_weight(w2, v2b)

    def ready(copies):
        for copy in copies:
            copy.wait()

    get_x.wait()

    def turn(x, carry):
        for z in range(DEPTH):
            wide[pl.ds(z, LENGTH, stride=DEPTH), :] = raw_x[x, z].astype(F32)
        e1[1 + x, pl.ds(1, LENGTH)] = wide[...].astype(BF).reshape(LENGTH, DEPTH, CH)
        return carry

    lax.fori_loop(0, ROWS, turn, 0)
    get_up.wait()
    cf[...] = jnp.zeros_like(cf)
    for qx in range(2):
        for qz in range(DEPTH // 2):
            cf[pl.ds(2 * qz, HALF, stride=DEPTH), :] = raw_up[qx, qz].astype(F32)
        eu[qx, 0:HALF] = cf[...].astype(BF).reshape(HALF, DEPTH, CH)
    pl.semaphore_wait(barrier, len(peers))

    in_x, in_y = pl.ds(1, ROWS), pl.ds(1, LENGTH)
    top, right = ROWS, LENGTH
    sides = [
        send(e1.at[in_x, right], e1.at[in_x, 0], near(0, 1)),
        send(e1.at[in_x, 1], e1.at[in_x, right + 1], near(0, -1)),
    ]
    below = [
        send(e1.at[top, right], e1.at[0, 0], near(1, 1)),
        send(e1.at[top, 1], e1.at[0, right + 1], near(1, -1)),
        send(e1.at[top, in_y], e1.at[0, in_y], near(1, 0)),
    ]
    above = [
        send(e1.at[1, right], e1.at[top + 1, 0], near(-1, 1)),
        send(e1.at[1, 1], e1.at[top + 1, right + 1], near(-1, -1)),
        send(e1.at[1, in_y], e1.at[top + 1, in_y], near(-1, 0)),
    ]
    due_one = {0: below, 1: sides, 2: [], 3: [], 4: [], top + 1: above}
    halo_up = [
        send(eu.at[0, pl.ds(0, HALF)], eu.at[2, pl.ds(0, HALF)], near(-1, 0)),
        send(eu.at[pl.ds(0, 2), 0], eu.at[pl.ds(0, 2), HALF], near(0, -1)),
        send(eu.at[0, 0], eu.at[2, HALF], near(-1, -1)),
    ]

    def arrived(copies):
        for copy in copies:
            copy.wait_recv()

    def clear(ref, row, width):
        rows, columns = ref.shape[0], ref.shape[1]
        line = jnp.zeros((columns, DEPTH, CH), BF)
        corner = jnp.zeros((width, DEPTH, CH), BF)
        if row < width:

            @pl.when(space == 0)
            def _():
                ref[row] = line

        if row >= rows - width:

            @pl.when(space == n_space - 1)
            def _():
                ref[row] = line

        @pl.when(chan == 0)
        def _():
            ref[row, 0:width] = corner

        @pl.when(chan == n_chan - 1)
        def _():
            ref[row, columns - width : columns] = corner

    def need(ref, due, width, *rows):
        for row in rows:
            if row in due:
                arrived(due.pop(row))
                clear(ref, row, width)

    def spread_row(ref, due, x):
        own = x + 2
        far, to = (own + ROWS, -1) if x < 2 else (own - ROWS, 1)
        first, last, y = pl.ds(2, 2), pl.ds(LENGTH, 2), pl.ds(2, LENGTH)
        before, after = pl.ds(0, 2), pl.ds(LENGTH + 2, 2)
        due[own] = [
            send(ref.at[own, last], ref.at[own, before], near(0, 1)),
            send(ref.at[own, first], ref.at[own, after], near(0, -1)),
        ]
        due[far] = [
            send(ref.at[own, last], ref.at[far, before], near(to, 1)),
            send(ref.at[own, first], ref.at[far, after], near(to, -1)),
            send(ref.at[own, y], ref.at[far, y], near(to, 0)),
        ]

    def flat(block):
        return block.reshape(-1, CH)

    def window(ref, x, begin, spread):
        return jnp.concatenate(
            [
                flat(ref[x + spread * ax, pl.ds(begin + spread * ay, HALF)])
                for ax in range(3)
                for ay in range(3)
            ],
            axis=1,
        )

    def fluid(half):
        depth = lax.broadcasted_iota(jnp.int32, (DEPTH, CH), 0)
        column = jnp.zeros((DEPTH, CH), jnp.int32)
        for i in range(DEPTH // TILE_Z):
            column = jnp.where(lax.div(depth, TILE_Z) == i, tiles[0, half, i], column)
        cells = jnp.broadcast_to(column.astype(F32)[None], (HALF, DEPTH, CH))
        return flat(cells)

    def taps_of(weight):
        blocks = [weight[ax, ay].reshape(WIDE, CH) for ax in range(3) for ay in range(3)]
        return jnp.concatenate(blocks, axis=1)

    def over(low, high, step):
        def one(i, carry):
            step(lax.div(i, 2), lax.rem(i, 2))
            return carry

        lax.fori_loop(low, high, one, 0)

    for qx in range(2):
        store_transposed(gt, qx, flat(eu[qx, 0:HALF]).astype(F32), 1)

    ready(get_v1f)

    def layer_one(x, half):
        pre = combined(matmul_transposed(window(e1, x, half * HALF, 1), taps_of(v1f)), 1, False)
        hidden, slope = gates(pre)
        inside = fluid(half)
        block = (hidden * inside).astype(BF).reshape(HALF, DEPTH, CH)
        e2[2 + x, pl.ds(2 + half * HALF, HALF)] = block
        d1[x, half] = slope * inside

    due_two, due_four = {}, {}
    need(e1, due_one, 1, 1, 2, 3, 4)
    over(2, 6, layer_one)
    spread_row(e2, due_two, 1)
    spread_row(e2, due_two, 2)
    need(e1, due_one, 1, 0)
    over(0, 2, layer_one)
    spread_row(e2, due_two, 0)
    need(e1, due_one, 1, top + 1)
    over(6, 8, layer_one)
    spread_row(e2, due_two, 3)

    arrived(halo_up)
    ready(get_v3b)

    @pl.when(space == n_space - 1)
    def _():
        eu[2] = jnp.zeros((HALF + 1, DEPTH, CH), BF)

    @pl.when(chan == n_chan - 1)
    def _():
        eu[:, HALF] = jnp.zeros((3, DEPTH, CH), BF)

    routes = (((1, 0),), ((0, 1), (2, 0)))
    for qx in range(2):
        for px in range(2):
            for py in range(2):
                taps = [(ax, dx, ay, dy) for ax, dx in routes[px] for ay, dy in routes[py]]
                cells = [flat(eu[qx + dx, dy : dy + HALF]) for _, dx, _, dy in taps]
                rows = [v3b[ax, ay] for ax, _, ay, _ in taps]
                if len(taps) > 1:
                    cells, rows = [jnp.concatenate(cells, axis=1)], [jnp.concatenate(rows, axis=0)]
                back = combined(matmul(cells[0], rows[0]), 1, True)
                b2[2 * qx + px, py] = back.astype(BF).reshape(HALF, DEPTH, CH)

    ready(get_v2f)

    def layer_two(x, half):
        pre = combined(matmul_transposed(window(e2, x, half * HALF, 2), taps_of(v2f)), 2, False)
        hidden, slope = gates(pre)
        inside = fluid(half)
        pairs = (hidden * inside).astype(BF).reshape(HALF // 2, 2, DEPTH, CH)
        first = half * (HALF // 2)
        e3[1 + x, 1, pl.ds(first, HALF // 2)] = pairs[:, 0]
        e3[1 + x, 0, pl.ds(first + 1, HALF // 2)] = pairs[:, 1]
        back = [b2[x, r, pl.ds(first, HALF // 2)].astype(F32) for r in range(2)]
        back = flat(jnp.stack(back, axis=1))
        product = (back * inside * slope).astype(BF)
        e4[2 + x, pl.ds(2 + half * HALF, HALF)] = product.reshape(HALF, DEPTH, CH)
        store_transposed(st, 2 * x + half, product.astype(F32), 2)

    evens, odds = pl.ds(0, HALF), pl.ds(1, HALF)
    inner = pl.ds(1, ROWS)
    halo_three = []
    for x in (3, 2, 1, 0):
        need(e2, due_two, 2, x, x + 2, x + 4)
        over(2 * x, 2 * x + 2, layer_two)
        spread_row(e4, due_four, x)
        if x == 3:
            halo_three += [
                send(e3.at[ROWS, 0, HALF], e3.at[0, 0, 0], near(1, 1)),
                send(e3.at[ROWS, 1, evens], e3.at[0, 1, evens], near(1, 0)),
                send(e3.at[ROWS, 0, odds], e3.at[0, 0, odds], near(1, 0)),
            ]
    halo_three.append(send(e3.at[inner, 0, HALF], e3.at[inner, 0, 0], near(0, 1)))

    waits = {}

    def place(k):
        if k < CHUNKS - 1:
            return k, slice(None)
        j = k - (CHUNKS - 1)
        return CHUNKS - 1, slice(j * CH, (j + 1) * CH)

    def share_core(k):
        b, w = place(k)
        cs[b, :, :, :, w] = part[b, :, :, 1 - core, :, w].astype(BF)
        waits[k] = [send(cs.at[b, :, :, :, w], cr.at[b, :, :, :, w], sibling)]

    def share_chan(k):
        b, w = place(k)
        arrived(waits[k])
        waits[k] = []
        for d in (2, 1, 3)[: n_chan - 1]:
            other = lax.rem(chan + d, n_chan)
            total = part[b, :, other, core, :, w] + cr[b, :, other, :, w].astype(F32)
            zs[b, d - 1, :, :, w] = total.astype(BF)
            block = (b, d - 1, slice(None), slice(None), w)
            waits[k].append(send(zs.at[block], zr.at[block], near(0, d)))

    def scatter(k, source, target, peer):
        b, w = place(k)
        waits[k] = [
            send(source.at[b, :, :, w], target.at[b, d - 1, :, :, w], peer(d)) for d in (2, 1, 3)
        ]

    def share_first(k):
        b, w = place(k)
        arrived(waits[k])
        total = part[b, :, chan, core, :, w] + cr[b, :, chan, :, w].astype(F32)
        for d in range(1, n_chan):
            total += zr[b, d - 1, :, :, w].astype(F32)
        xs[b, :, :, w] = total.astype(BF)
        scatter(k, xs, xr, (x_peer, y_peer)[k % 2])

    def four(own, others, k):
        b, w = place(k)
        opposite = own[b, :, :, w].astype(F32) + others[b, 1, :, :, w].astype(F32)
        return opposite + (others[b, 0, :, :, w].astype(F32) + others[b, 2, :, :, w].astype(F32))

    def share_second(k):
        b, w = place(k)
        arrived(waits[k])
        ys[b, :, :, w] = four(xs, xr, k).astype(BF)
        scatter(k, ys, yr, (y_peer, x_peer)[k % 2])

    def share_back(k):
        b, w = place(k)
        arrived(waits[k])
        fs[b, :, :, w] = four(ys, yr, k)
        waits[k] = [send(fs.at[b, :, :, w], fr.at[b, :, :, w], sibling)]

    def finish(k):
        b, _ = place(k)
        arrived(waits[k])
        out = (out2, out3, out1)[b // 3]
        for ay in range(3) if b == k and k < CHUNKS - 1 else (k - CHUNKS + 1,):
            columns = slice(ay * CH, (ay + 1) * CH)
            out[b % 3, :, ay, core] = fs[b, :, :, columns]
            out[b % 3, :, ay, 1 - core] = fr[b, :, :, columns]

    stages = (share_core, share_chan, share_first, share_second, share_back, finish)
    progress = {}

    def advance(*chunks):
        for k in chunks:
            at = progress.get(k, 0)
            if at < len(stages):
                stages[at](k)
                progress[k] = at + 1

    def grads(k, ref, spread):
        ax = k % 3
        slopes = jnp.concatenate([st[i] for i in range(2 * ROWS)], axis=1)
        cells = jnp.concatenate(
            [
                jnp.concatenate(
                    [
                        flat(ref[x + spread * ax, spread * ay : spread * ay + LENGTH])
                        for ay in range(3)
                    ],
                    axis=1,
                )
                for x in range(ROWS)
            ],
            axis=0,
        )
        part[k] = matmul(slopes, cells).reshape(part.shape[1:])

    def coarse_window(x):
        return [flat(e3[x, r, j : j + HALF]) for r, j in ((0, 0), (1, 0), (0, 1))]

    def coarse_grads(k):
        ax = k % 3
        total = 0.0
        for qx in range(2):
            cells = jnp.concatenate(coarse_window(2 * qx + ax), axis=1)
            total += matmul(gt[qx], cells)
        part[k] = total.reshape(part.shape[1:])

    grads(0, e2, 2)
    advance(0)
    grads(1, e2, 2)
    advance(1)
    grads(2, e2, 2)
    advance(2, 0)
    arrived(halo_three)
    ready(get_v3f)

    @pl.when(space == 0)
    def _():
        e3[0] = jnp.zeros(e3.shape[1:], BF)

    @pl.when(chan == 0)
    def _():
        e3[:, 0, 0] = jnp.zeros((ROWS + 1, DEPTH, CH), BF)

    for k in range(3, 6):
        coarse_grads(k)
        advance(k)

    def coarse_rows(qx):
        cells = [block for ax in range(3) for block in coarse_window(2 * qx + ax)]
        cells = jnp.concatenate(cells, axis=1)
        cf[...] = combined(matmul_transposed(cells, taps_of(v3f)), 1, False)
        for qz in range(DEPTH // 2):
            coarse[qx, qz] = cf[pl.ds(2 * qz, HALF, stride=DEPTH), :].astype(BF)

    advance(1)
    ready(get_v2b)

    def layer_back(x, half):
        back = combined(matmul(mirror(x, half), v2b[...].reshape(TAPS, WIDE)), 2, True).astype(BF).astype(F32)
        slope = (back * d1[x, half]).astype(BF)
        store_transposed(st, 2 * x + half, slope.astype(F32), 1)

    def mirror(x, half):
        return jnp.concatenate(
            [
                flat(e4[x + 4 - 2 * ax, pl.ds(half * HALF + 4 - 2 * ay, HALF)])
                for ax in range(3)
                for ay in range(3)
            ],
            axis=1,
        )

    for x in (1, 0, 3, 2):
        need(e4, due_four, 2, x, x + 2, x + 4)
        over(2 * x, 2 * x + 2, layer_back)
        advance(*((2, 0) if x in (1, 3) else (3, 4, 5, 1)))
    grads(6, e1, 1)
    advance(6, 2, 0)
    grads(7, e1, 1)
    advance(7, 3, 4, 5)
    grads(8, e1, 1)
    advance(8, 9, 10, 6, 1)
    coarse_rows(0)
    advance(7, 0, 2)
    coarse_rows(1)
    advance(8, 9, 10, 3, 4, 5, 6, 1, 7, 2)
    last = (6, 7, 8, 9, 10)
    advance(8, 9, 10, 6, 3, 4, 5, 7)
    while any(progress[k] < len(stages) for k in last):
        advance(*last)
    for copy in started:
        copy.wait_send()


def write_out(*refs):
    sources, targets, staged, sems = refs[:4], refs[4:8], refs[8:12], refs[12]
    loads = [
        pltpu.make_async_copy(a, b, sems.at[i]) for i, (a, b) in enumerate(zip(sources, staged))
    ]
    stores = [
        pltpu.make_async_copy(a, b, sems.at[4 + i]) for i, (a, b) in enumerate(zip(staged, targets))
    ]
    for copy in loads:
        copy.start()
    for load, store in zip(loads, stores):
        load.wait()
        store.start()
    for copy in stores:
        copy.wait()


def local(features, fluid_tiles, weight_one, weight_two, weight_three, upstream, sizes):
    n_space, n_chan = sizes
    tiles = jnp.transpose(fluid_tiles, (0, 2, 1))

    def by_tap(weight):
        return jnp.transpose(weight, (1, 2, 3, 0, 4))

    def by_output(grad):
        return jnp.transpose(grad.reshape(3, 3, 3, 2 * 16, CH), (3, 0, 1, 2, 4))

    hbm = pl.BlockSpec(memory_space=pl.ANY)
    vmem = pl.BlockSpec(memory_space=pltpu.VMEM)
    smem = pl.BlockSpec(memory_space=pltpu.SMEM)
    grad_shape = jax.ShapeDtypeStruct((3, 3, 3, 2, 16, CH), F32)
    copies = 55 + 11 * (CHUNKS + 2)
    forward_shape = pltpu.VMEM((3, 3, 3, CH, CH), BF)
    backward_shape = pltpu.VMEM((3, 3, CH, WIDE), BF)
    piece = (CHUNKS, 3, 16, WIDE)
    pieces = (CHUNKS, 3, 3, 16, WIDE)
    results = pl.pallas_call(
        functools.partial(program, n_space, n_chan),
        out_shape=(
            jax.ShapeDtypeStruct((2, DEPTH // 2, HALF, CH), BF),
            grad_shape,
            grad_shape,
            grad_shape,
        ),
        in_specs=[hbm, hbm, smem, hbm, hbm, hbm],
        out_specs=[vmem] * 4,
        scratch_shapes=[
            pltpu.VMEM((ROWS + 2, LENGTH + 2, DEPTH, CH), BF),
            pltpu.VMEM((ROWS + 4, LENGTH + 4, DEPTH, CH), BF),
            pltpu.VMEM((ROWS + 1, 2, HALF + 1, DEPTH, CH), BF),
            pltpu.VMEM((ROWS + 4, LENGTH + 4, DEPTH, CH), BF),
            pltpu.VMEM((3, HALF + 1, DEPTH, CH), BF),
            pltpu.VMEM((ROWS, 2, CELLS, CH), F32),
            pltpu.VMEM((ROWS, 2, HALF, DEPTH, CH), BF),
            forward_shape,
            forward_shape,
            forward_shape,
            backward_shape,
            backward_shape,
            pltpu.VMEM((8, WIDE, CELLS), BF),
            pltpu.VMEM((2, WIDE, CELLS), BF),
            pltpu.VMEM((CELLS, CH), F32),
            pltpu.VMEM((ROWS, DEPTH, LENGTH, CH), BF),
            pltpu.VMEM((2, DEPTH // 2, HALF, CH), BF),
            pltpu.VMEM((LENGTH * DEPTH, CH), F32),
            pltpu.VMEM((CHUNKS, 3, n_chan, 2, 16, WIDE), F32),
            pltpu.VMEM((CHUNKS, 3, n_chan, 16, WIDE), BF),
            pltpu.VMEM((CHUNKS, 3, n_chan, 16, WIDE), BF),
            pltpu.VMEM(pieces, BF),
            pltpu.VMEM(pieces, BF),
            pltpu.VMEM(piece, BF),
            pltpu.VMEM(pieces, BF),
            pltpu.VMEM(piece, BF),
            pltpu.VMEM(pieces, BF),
            pltpu.VMEM(piece, F32),
            pltpu.VMEM(piece, F32),
            pltpu.SemaphoreType.DMA((copies,)),
            pltpu.SemaphoreType.DMA((copies,)),
            pltpu.SemaphoreType.DMA((17,)),
        ],
        compiler_params=pltpu.CompilerParams(
            collective_id=0, has_side_effects=True, vmem_limit_bytes=58 << 20
        ),
    )(
        features,
        upstream,
        tiles,
        by_tap(weight_one),
        by_tap(weight_two),
        by_tap(weight_three),
    )
    coarse, grad_one, grad_two, grad_three = pl.pallas_call(
        write_out,
        out_shape=tuple(jax.ShapeDtypeStruct(r.shape, r.dtype) for r in results),
        in_specs=[hbm] * 4,
        out_specs=[hbm] * 4,
        scratch_shapes=[pltpu.VMEM(r.shape, r.dtype) for r in results]
        + [pltpu.SemaphoreType.DMA((8,))],
    )(*results)
    return coarse, by_output(grad_one), by_output(grad_two), by_output(grad_three)


def solution(mesh):
    in_specs = (
        P("space", None, "chan", None),
        P("space", None, "chan"),
        P(),
        P(),
        P(),
        P("space", None, "chan", None),
    )
    out_specs = (
        P("space", None, "chan", None),
        P("chan", None, None, None, None),
        P("chan", None, None, None, None),
        P("chan", None, None, None, None),
    )
    sizes = (mesh.shape["space"], mesh.shape["chan"])
    return jax.shard_map(
        functools.partial(local, sizes=sizes),
        mesh=mesh,
        in_specs=in_specs,
        out_specs=out_specs,
        check_vma=False,
    )
```

```python
import functools

import jax
import jax.numpy as jnp
from jax import lax
from jax.experimental import pallas as pl
from jax.experimental.pallas import tpu as pltpu
from jax.sharding import PartitionSpec as P

TILE_Z = 4
TILE_Y = 32
ROWS = 4
LENGTH = 64
DEPTH = 16
CH = 128
HALF = LENGTH // 2
CELLS = HALF * DEPTH
TAPS = 9 * CH
WIDE = 3 * CH
CHIPS = 4
CHUNKS = 9
BF = jnp.bfloat16
F32 = jnp.float32
MESH = pl.DeviceIdType.MESH


def matmul_transposed(left, right):
    return lax.dot_general(left, right, (((1,), (1,)), ((), ())), preferred_element_type=F32)


def matmul(left, right):
    return jnp.dot(left, right, preferred_element_type=F32)


def depth_of(shape, axis):
    return lax.broadcasted_iota(jnp.int32, shape, axis) & (DEPTH - 1)


def rotated(values, step):
    turned = pltpu.roll(values.reshape(-1, 8, CH), step, 1)
    return turned.reshape(-1, 2, 8, CH)


def combined(wide, step, mirrored):
    first, middle, last = (wide[:, i * CH : (i + 1) * CH] for i in range(3))
    if mirrored:
        first, last = last, first
    depth = lax.broadcasted_iota(jnp.int32, (1, 8, CH), 1)
    low, high = depth < step, depth >= 8 - step
    down, up = rotated(first, step), rotated(last, 8 - step)
    upper = jnp.where(low, 0.0, down[:, 0]) + jnp.where(high, up[:, 1], up[:, 0])
    lower = jnp.where(low, down[:, 0], down[:, 1]) + jnp.where(high, 0.0, up[:, 1])
    return middle + jnp.stack([upper, lower], axis=1).reshape(-1, CH)


def store_transposed(target, slot, values, step):
    depth = depth_of((CH, CH), 1)
    for j in range(values.shape[0] // CH):
        block = jnp.transpose(values[j * CH : (j + 1) * CH, :])
        ahead = jnp.where(depth < DEPTH - step, pltpu.roll(block, CH - step, 1), 0.0)
        behind = jnp.where(depth >= step, pltpu.roll(block, step, 1), 0.0)
        columns = slice(j * CH, (j + 1) * CH)
        target[slot, 0:CH, columns] = ahead.astype(BF)
        target[slot, CH : 2 * CH, columns] = block.astype(BF)
        target[slot, 2 * CH : 3 * CH, columns] = behind.astype(BF)


def gates(values):
    sigma = 0.5 * jnp.tanh(0.5 * values) + 0.5
    return values * sigma, sigma * (1.0 + values * (1.0 - sigma))


def program(
    n_space,
    n_chan,
    feat,
    up,
    tiles,
    w1,
    w2,
    w3,
    coarse,
    out1,
    out2,
    out3,
    e1,
    e2,
    e3,
    e4,
    eu,
    d1,
    b2,
    v1f,
    v2f,
    v3f,
    v2b,
    v3b,
    st,
    gt,
    cf,
    raw_x,
    raw_up,
    wide,
    part,
    cs,
    cr,
    zs,
    zr,
    xs,
    xr,
    ys,
    yr,
    fs,
    fr,
    send_sem,
    recv_sem,
    local_sem,
):
    space = lax.axis_index("space")
    chan = lax.axis_index("chan")
    core = lax.rem(space, 2)
    chip_x = lax.rem(lax.div(space, 2), CHIPS)
    chip_y = lax.div(space, 2 * CHIPS)

    def near(d_space, d_chan):
        return (
            lax.rem(space + (d_space + n_space), n_space),
            lax.rem(chan + (d_chan + n_chan), n_chan),
        )

    sibling = (space + 1 - 2 * core, chan)

    def x_peer(d):
        return (chip_y * (2 * CHIPS) + lax.rem(chip_x + d, CHIPS) * 2 + core, chan)

    def y_peer(d):
        return (lax.rem(chip_y + d, CHIPS) * (2 * CHIPS) + chip_x * 2 + core, chan)

    started = []

    def send(source, target, device):
        index = len(started)
        copy = pltpu.make_async_remote_copy(
            src_ref=source,
            dst_ref=target,
            send_sem=send_sem.at[index],
            recv_sem=recv_sem.at[index],
            device_id=device,
            device_id_type=MESH,
        )
        copy.start()
        started.append(copy)
        return copy

    local = []

    def fetch(source, target):
        copy = pltpu.make_async_copy(source, target, local_sem.at[len(local)])
        copy.start()
        local.append(copy)
        return copy

    peers = [near(a, b) for a in (-1, 0, 1) for b in (-1, 0, 1) if (a, b) != (0, 0)]
    peers.append(near(0, 2))
    peers += [x_peer(d) for d in range(1, CHIPS)]
    peers += [y_peer(d) for d in range(1, CHIPS)]
    barrier = pltpu.get_barrier_semaphore()
    for peer in peers:
        pl.semaphore_signal(barrier, inc=1, device_id=peer, device_id_type=MESH)
    get_x = fetch(feat, raw_x)
    get_up = fetch(up, raw_up)

    def forward_weight(source, target):
        return [fetch(source.at[:, az], target.at[:, :, az]) for az in range(3)]

    def backward_weight(source, target):
        return [
            fetch(source.at[:, az], target.at[:, :, :, az * CH : (az + 1) * CH])
            for az in range(3)
        ]

    get_v1f = forward_weight(w1, v1f)
    get_v3b = backward_weight(w3, v3b)
    get_v2f = forward_weight(w2, v2f)
    get_v3f = forward_weight(w3, v3f)
    get_v2b = backward_weight(w2, v2b)

    def ready(copies):
        for copy in copies:
            copy.wait()

    get_x.wait()

    def turn(x, carry):
        for z in range(DEPTH):
            wide[pl.ds(z, LENGTH, stride=DEPTH), :] = raw_x[x, z].astype(F32)
        e1[1 + x, pl.ds(1, LENGTH)] = wide[...].astype(BF).reshape(LENGTH, DEPTH, CH)
        return carry

    lax.fori_loop(0, ROWS, turn, 0)
    get_up.wait()
    cf[...] = jnp.zeros_like(cf)
    for qx in range(2):
        for qz in range(DEPTH // 2):
            cf[pl.ds(2 * qz, HALF, stride=DEPTH), :] = raw_up[qx, qz].astype(F32)
        eu[qx, 0:HALF] = cf[...].astype(BF).reshape(HALF, DEPTH, CH)
    pl.semaphore_wait(barrier, len(peers))

    in_x, in_y = pl.ds(1, ROWS), pl.ds(1, LENGTH)
    top, right = ROWS, LENGTH
    sides = [
        send(e1.at[in_x, right], e1.at[in_x, 0], near(0, 1)),
        send(e1.at[in_x, 1], e1.at[in_x, right + 1], near(0, -1)),
    ]
    below = [
        send(e1.at[top, right], e1.at[0, 0], near(1, 1)),
        send(e1.at[top, 1], e1.at[0, right + 1], near(1, -1)),
        send(e1.at[top, in_y], e1.at[0, in_y], near(1, 0)),
    ]
    above = [
        send(e1.at[1, right], e1.at[top + 1, 0], near(-1, 1)),
        send(e1.at[1, 1], e1.at[top + 1, right + 1], near(-1, -1)),
        send(e1.at[1, in_y], e1.at[top + 1, in_y], near(-1, 0)),
    ]
    due_one = {0: below, 1: sides, 2: [], 3: [], 4: [], top + 1: above}
    halo_up = [
        send(eu.at[0, pl.ds(0, HALF)], eu.at[2, pl.ds(0, HALF)], near(-1, 0)),
        send(eu.at[pl.ds(0, 2), 0], eu.at[pl.ds(0, 2), HALF], near(0, -1)),
        send(eu.at[0, 0], eu.at[2, HALF], near(-1, -1)),
    ]

    def arrived(copies):
        for copy in copies:
            copy.wait_recv()

    def clear(ref, row, width):
        rows, columns = ref.shape[0], ref.shape[1]
        line = jnp.zeros((columns, DEPTH, CH), BF)
        corner = jnp.zeros((width, DEPTH, CH), BF)
        if row < width:

            @pl.when(space == 0)
            def _():
                ref[row] = line

        if row >= rows - width:

            @pl.when(space == n_space - 1)
            def _():
                ref[row] = line

        @pl.when(chan == 0)
        def _():
            ref[row, 0:width] = corner

        @pl.when(chan == n_chan - 1)
        def _():
            ref[row, columns - width : columns] = corner

    def need(ref, due, width, *rows):
        for row in rows:
            if row in due:
                arrived(due.pop(row))
                clear(ref, row, width)

    def spread_row(ref, due, x):
        own = x + 2
        far, to = (own + ROWS, -1) if x < 2 else (own - ROWS, 1)
        first, last, y = pl.ds(2, 2), pl.ds(LENGTH, 2), pl.ds(2, LENGTH)
        before, after = pl.ds(0, 2), pl.ds(LENGTH + 2, 2)
        due[own] = [
            send(ref.at[own, last], ref.at[own, before], near(0, 1)),
            send(ref.at[own, first], ref.at[own, after], near(0, -1)),
        ]
        due[far] = [
            send(ref.at[own, last], ref.at[far, before], near(to, 1)),
            send(ref.at[own, first], ref.at[far, after], near(to, -1)),
            send(ref.at[own, y], ref.at[far, y], near(to, 0)),
        ]

    def flat(block):
        return block.reshape(-1, CH)

    def window(ref, x, begin, spread):
        return jnp.concatenate(
            [
                flat(ref[x + spread * ax, pl.ds(begin + spread * ay, HALF)])
                for ax in range(3)
                for ay in range(3)
            ],
            axis=1,
        )

    def fluid(half):
        depth = lax.broadcasted_iota(jnp.int32, (DEPTH, CH), 0)
        column = jnp.zeros((DEPTH, CH), jnp.int32)
        for i in range(DEPTH // TILE_Z):
            column = jnp.where(lax.div(depth, TILE_Z) == i, tiles[0, half, i], column)
        cells = jnp.broadcast_to(column.astype(F32)[None], (HALF, DEPTH, CH))
        return flat(cells)

    def taps_of(weight):
        blocks = [weight[ax, ay].reshape(WIDE, CH) for ax in range(3) for ay in range(3)]
        return jnp.concatenate(blocks, axis=1)

    def over(low, high, step):
        def one(i, carry):
            step(lax.div(i, 2), lax.rem(i, 2))
            return carry

        lax.fori_loop(low, high, one, 0)

    for qx in range(2):
        store_transposed(gt, qx, flat(eu[qx, 0:HALF]).astype(F32), 1)

    ready(get_v1f)

    def layer_one(x, half):
        pre = combined(matmul_transposed(window(e1, x, half * HALF, 1), taps_of(v1f)), 1, False)
        hidden, slope = gates(pre)
        inside = fluid(half)
        block = (hidden * inside).astype(BF).reshape(HALF, DEPTH, CH)
        e2[2 + x, pl.ds(2 + half * HALF, HALF)] = block
        d1[x, half] = slope * inside

    due_two, due_four = {}, {}
    need(e1, due_one, 1, 1, 2, 3, 4)
    over(2, 6, layer_one)
    spread_row(e2, due_two, 1)
    spread_row(e2, due_two, 2)
    need(e1, due_one, 1, 0)
    over(0, 2, layer_one)
    spread_row(e2, due_two, 0)
    need(e1, due_one, 1, top + 1)
    over(6, 8, layer_one)
    spread_row(e2, due_two, 3)

    arrived(halo_up)
    ready(get_v3b)

    @pl.when(space == n_space - 1)
    def _():
        eu[2] = jnp.zeros((HALF + 1, DEPTH, CH), BF)

    @pl.when(chan == n_chan - 1)
    def _():
        eu[:, HALF] = jnp.zeros((3, DEPTH, CH), BF)

    routes = (((1, 0),), ((0, 1), (2, 0)))
    for qx in range(2):
        for px in range(2):
            for py in range(2):
                taps = [(ax, dx, ay, dy) for ax, dx in routes[px] for ay, dy in routes[py]]
                cells = [flat(eu[qx + dx, dy : dy + HALF]) for _, dx, _, dy in taps]
                rows = [v3b[ax, ay] for ax, _, ay, _ in taps]
                if len(taps) > 1:
                    cells, rows = [jnp.concatenate(cells, axis=1)], [jnp.concatenate(rows, axis=0)]
                back = combined(matmul(cells[0], rows[0]), 1, True)
                b2[2 * qx + px, py] = back.astype(BF).reshape(HALF, DEPTH, CH)

    ready(get_v2f)

    def layer_two(x, half):
        pre = combined(matmul_transposed(window(e2, x, half * HALF, 2), taps_of(v2f)), 2, False)
        hidden, slope = gates(pre)
        inside = fluid(half)
        pairs = (hidden * inside).astype(BF).reshape(HALF // 2, 2, DEPTH, CH)
        first = half * (HALF // 2)
        e3[1 + x, 1, pl.ds(first, HALF // 2)] = pairs[:, 0]
        e3[1 + x, 0, pl.ds(first + 1, HALF // 2)] = pairs[:, 1]
        back = [b2[x, r, pl.ds(first, HALF // 2)].astype(F32) for r in range(2)]
        back = flat(jnp.stack(back, axis=1))
        product = (back * inside * slope).astype(BF)
        e4[2 + x, pl.ds(2 + half * HALF, HALF)] = product.reshape(HALF, DEPTH, CH)
        store_transposed(st, 2 * x + half, product.astype(F32), 2)

    evens, odds = pl.ds(0, HALF), pl.ds(1, HALF)
    inner = pl.ds(1, ROWS)
    halo_three = []
    for x in (3, 2, 1, 0):
        need(e2, due_two, 2, x, x + 2, x + 4)
        over(2 * x, 2 * x + 2, layer_two)
        spread_row(e4, due_four, x)
        if x == 3:
            halo_three += [
                send(e3.at[ROWS, 0, HALF], e3.at[0, 0, 0], near(1, 1)),
                send(e3.at[ROWS, 1, evens], e3.at[0, 1, evens], near(1, 0)),
                send(e3.at[ROWS, 0, odds], e3.at[0, 0, odds], near(1, 0)),
            ]
    halo_three.append(send(e3.at[inner, 0, HALF], e3.at[inner, 0, 0], near(0, 1)))

    waits = {}

    def place(k):
        if k < CHUNKS - 1:
            return k, slice(None)
        j = k - (CHUNKS - 1)
        return CHUNKS - 1, slice(j * CH, (j + 1) * CH)

    def share_core(k):
        b, w = place(k)
        cs[b, :, :, :, w] = part[b, :, :, 1 - core, :, w].astype(BF)
        waits[k] = [send(cs.at[b, :, :, :, w], cr.at[b, :, :, :, w], sibling)]

    def share_chan(k):
        b, w = place(k)
        arrived(waits[k])
        waits[k] = []
        for d in (2, 1, 3)[: n_chan - 1]:
            other = lax.rem(chan + d, n_chan)
            total = part[b, :, other, core, :, w] + cr[b, :, other, :, w].astype(F32)
            zs[b, d - 1, :, :, w] = total.astype(BF)
            block = (b, d - 1, slice(None), slice(None), w)
            waits[k].append(send(zs.at[block], zr.at[block], near(0, d)))

    def scatter(k, source, target, peer):
        b, w = place(k)
        waits[k] = [
            send(source.at[b, :, :, w], target.at[b, d - 1, :, :, w], peer(d)) for d in (2, 1, 3)
        ]

    def share_first(k):
        b, w = place(k)
        arrived(waits[k])
        total = part[b, :, chan, core, :, w] + cr[b, :, chan, :, w].astype(F32)
        for d in range(1, n_chan):
            total += zr[b, d - 1, :, :, w].astype(F32)
        xs[b, :, :, w] = total.astype(BF)
        scatter(k, xs, xr, (x_peer, y_peer)[k % 2])

    def four(own, others, k):
        b, w = place(k)
        opposite = own[b, :, :, w].astype(F32) + others[b, 1, :, :, w].astype(F32)
        return opposite + (others[b, 0, :, :, w].astype(F32) + others[b, 2, :, :, w].astype(F32))

    def share_second(k):
        b, w = place(k)
        arrived(waits[k])
        ys[b, :, :, w] = four(xs, xr, k).astype(BF)
        scatter(k, ys, yr, (y_peer, x_peer)[k % 2])

    def share_back(k):
        b, w = place(k)
        arrived(waits[k])
        fs[b, :, :, w] = four(ys, yr, k)
        waits[k] = [send(fs.at[b, :, :, w], fr.at[b, :, :, w], sibling)]

    def finish(k):
        b, _ = place(k)
        arrived(waits[k])
        out = (out2, out3, out1)[b // 3]
        for ay in range(3) if b == k and k < CHUNKS - 1 else (k - CHUNKS + 1,):
            columns = slice(ay * CH, (ay + 1) * CH)
            out[b % 3, :, ay, core] = fs[b, :, :, columns]
            out[b % 3, :, ay, 1 - core] = fr[b, :, :, columns]

    left = []

    def sent(keep):
        while len(left) < len(started) - keep:
            copy = started[len(left)]
            copy.wait_send()
            left.append(copy)

    stages = (share_core, share_chan, share_first, share_second, share_back, finish)
    progress = {}

    def advance(*chunks):
        for k in chunks:
            at = progress.get(k, 0)
            if at < len(stages):
                stages[at](k)
                progress[k] = at + 1

    def grads(k, ref, spread):
        ax = k % 3
        slopes = jnp.concatenate([st[i] for i in range(2 * ROWS)], axis=1)
        cells = jnp.concatenate(
            [
                jnp.concatenate(
                    [
                        flat(ref[x + spread * ax, spread * ay : spread * ay + LENGTH])
                        for ay in range(3)
                    ],
                    axis=1,
                )
                for x in range(ROWS)
            ],
            axis=0,
        )
        part[k] = matmul(slopes, cells).reshape(part.shape[1:])

    def coarse_window(x):
        return [flat(e3[x, r, j : j + HALF]) for r, j in ((0, 0), (1, 0), (0, 1))]

    def coarse_grads(k):
        ax = k % 3
        total = 0.0
        for qx in range(2):
            cells = jnp.concatenate(coarse_window(2 * qx + ax), axis=1)
            total += matmul(gt[qx], cells)
        part[k] = total.reshape(part.shape[1:])

    grads(0, e2, 2)
    advance(0)
    grads(1, e2, 2)
    advance(1)
    grads(2, e2, 2)
    advance(2, 0)
    arrived(halo_three)
    ready(get_v3f)

    @pl.when(space == 0)
    def _():
        e3[0] = jnp.zeros(e3.shape[1:], BF)

    @pl.when(chan == 0)
    def _():
        e3[:, 0, 0] = jnp.zeros((ROWS + 1, DEPTH, CH), BF)

    for k in range(3, 6):
        coarse_grads(k)
        advance(k)

    def coarse_rows(qx):
        cells = [block for ax in range(3) for block in coarse_window(2 * qx + ax)]
        cells = jnp.concatenate(cells, axis=1)
        cf[...] = combined(matmul_transposed(cells, taps_of(v3f)), 1, False)
        for qz in range(DEPTH // 2):
            coarse[qx, qz] = cf[pl.ds(2 * qz, HALF, stride=DEPTH), :].astype(BF)

    advance(1)
    ready(get_v2b)

    def layer_back(x, half):
        back = combined(matmul(mirror(x, half), v2b[...].reshape(TAPS, WIDE)), 2, True).astype(BF).astype(F32)
        slope = (back * d1[x, half]).astype(BF)
        store_transposed(st, 2 * x + half, slope.astype(F32), 1)

    def mirror(x, half):
        return jnp.concatenate(
            [
                flat(e4[x + 4 - 2 * ax, pl.ds(half * HALF + 4 - 2 * ay, HALF)])
                for ax in range(3)
                for ay in range(3)
            ],
            axis=1,
        )

    for x in (1, 0, 3, 2):
        need(e4, due_four, 2, x, x + 2, x + 4)
        over(2 * x, 2 * x + 2, layer_back)
        advance(*((2, 0) if x in (1, 3) else (3, 4, 5, 1)))
    grads(6, e1, 1)
    advance(6, 2, 0)
    grads(7, e1, 1)
    advance(7, 3, 4, 5)
    grads(8, e1, 1)
    advance(8, 9, 10, 6, 1)
    coarse_rows(0)
    advance(8, 9, 10, 7, 0, 2)
    coarse_rows(1)
    sent(60)
    advance(8, 9, 10, 6, 7)
    advance(3, 4, 5, 1, 2)
    sent(40)
    advance(8, 9, 10, 6, 7)
    advance(3, 4, 5)
    sent(24)
    advance(8, 9, 10, 6, 7)
    sent(12)
    advance(6, 7, 8, 9, 10)
    sent(0)
    assert all(progress[k] == len(stages) for k in range(CHUNKS + 2))


def write_out(*refs):
    sources, targets, staged, sems = refs[:4], refs[4:8], refs[8:12], refs[12]
    loads = [
        pltpu.make_async_copy(a, b, sems.at[i]) for i, (a, b) in enumerate(zip(sources, staged))
    ]
    stores = [
        pltpu.make_async_copy(a, b, sems.at[4 + i]) for i, (a, b) in enumerate(zip(staged, targets))
    ]
    for copy in loads:
        copy.start()
    for load, store in zip(loads, stores):
        load.wait()
        store.start()
    for copy in stores:
        copy.wait()


def local(features, fluid_tiles, weight_one, weight_two, weight_three, upstream, sizes):
    n_space, n_chan = sizes
    tiles = jnp.transpose(fluid_tiles, (0, 2, 1))

    def by_tap(weight):
        return jnp.transpose(weight, (1, 2, 3, 0, 4))

    def by_output(grad):
        return jnp.transpose(grad.reshape(3, 3, 3, 2 * 16, CH), (3, 0, 1, 2, 4))

    hbm = pl.BlockSpec(memory_space=pl.ANY)
    vmem = pl.BlockSpec(memory_space=pltpu.VMEM)
    smem = pl.BlockSpec(memory_space=pltpu.SMEM)
    grad_shape = jax.ShapeDtypeStruct((3, 3, 3, 2, 16, CH), F32)
    copies = 55 + 11 * (CHUNKS + 2)
    forward_shape = pltpu.VMEM((3, 3, 3, CH, CH), BF)
    backward_shape = pltpu.VMEM((3, 3, CH, WIDE), BF)
    piece = (CHUNKS, 3, 16, WIDE)
    pieces = (CHUNKS, 3, 3, 16, WIDE)
    results = pl.pallas_call(
        functools.partial(program, n_space, n_chan),
        out_shape=(
            jax.ShapeDtypeStruct((2, DEPTH // 2, HALF, CH), BF),
            grad_shape,
            grad_shape,
            grad_shape,
        ),
        in_specs=[hbm, hbm, smem, hbm, hbm, hbm],
        out_specs=[vmem] * 4,
        scratch_shapes=[
            pltpu.VMEM((ROWS + 2, LENGTH + 2, DEPTH, CH), BF),
            pltpu.VMEM((ROWS + 4, LENGTH + 4, DEPTH, CH), BF),
            pltpu.VMEM((ROWS + 1, 2, HALF + 1, DEPTH, CH), BF),
            pltpu.VMEM((ROWS + 4, LENGTH + 4, DEPTH, CH), BF),
            pltpu.VMEM((3, HALF + 1, DEPTH, CH), BF),
            pltpu.VMEM((ROWS, 2, CELLS, CH), F32),
            pltpu.VMEM((ROWS, 2, HALF, DEPTH, CH), BF),
            forward_shape,
            forward_shape,
            forward_shape,
            backward_shape,
            backward_shape,
            pltpu.VMEM((8, WIDE, CELLS), BF),
            pltpu.VMEM((2, WIDE, CELLS), BF),
            pltpu.VMEM((CELLS, CH), F32),
            pltpu.VMEM((ROWS, DEPTH, LENGTH, CH), BF),
            pltpu.VMEM((2, DEPTH // 2, HALF, CH), BF),
            pltpu.VMEM((LENGTH * DEPTH, CH), F32),
            pltpu.VMEM((CHUNKS, 3, n_chan, 2, 16, WIDE), F32),
            pltpu.VMEM((CHUNKS, 3, n_chan, 16, WIDE), BF),
            pltpu.VMEM((CHUNKS, 3, n_chan, 16, WIDE), BF),
            pltpu.VMEM(pieces, BF),
            pltpu.VMEM(pieces, BF),
            pltpu.VMEM(piece, BF),
            pltpu.VMEM(pieces, BF),
            pltpu.VMEM(piece, BF),
            pltpu.VMEM(pieces, BF),
            pltpu.VMEM(piece, F32),
            pltpu.VMEM(piece, F32),
            pltpu.SemaphoreType.DMA((copies,)),
            pltpu.SemaphoreType.DMA((copies,)),
            pltpu.SemaphoreType.DMA((17,)),
        ],
        compiler_params=pltpu.CompilerParams(
            collective_id=0, has_side_effects=True, vmem_limit_bytes=58 << 20
        ),
    )(
        features,
        upstream,
        tiles,
        by_tap(weight_one),
        by_tap(weight_two),
        by_tap(weight_three),
    )
    coarse, grad_one, grad_two, grad_three = pl.pallas_call(
        write_out,
        out_shape=tuple(jax.ShapeDtypeStruct(r.shape, r.dtype) for r in results),
        in_specs=[hbm] * 4,
        out_specs=[hbm] * 4,
        scratch_shapes=[pltpu.VMEM(r.shape, r.dtype) for r in results]
        + [pltpu.SemaphoreType.DMA((8,))],
    )(*results)
    return coarse, by_output(grad_one), by_output(grad_two), by_output(grad_three)


def solution(mesh):
    in_specs = (
        P("space", None, "chan", None),
        P("space", None, "chan"),
        P(),
        P(),
        P(),
        P("space", None, "chan", None),
    )
    out_specs = (
        P("space", None, "chan", None),
        P("chan", None, None, None, None),
        P("chan", None, None, None, None),
        P("chan", None, None, None, None),
    )
    sizes = (mesh.shape["space"], mesh.shape["chan"])
    return jax.shard_map(
        functools.partial(local, sizes=sizes),
        mesh=mesh,
        in_specs=in_specs,
        out_specs=out_specs,
        check_vma=False,
    )
```

```python
import functools

import jax
import jax.numpy as jnp
from jax import lax
from jax.experimental import pallas as pl
from jax.experimental.pallas import tpu as pltpu
from jax.sharding import PartitionSpec as P

TILE_Z = 4
TILE_Y = 32
ROWS = 4
LENGTH = 64
DEPTH = 16
CH = 128
HALF = LENGTH // 2
CELLS = HALF * DEPTH
TAPS = 9 * CH
WIDE = 3 * CH
CHIPS = 4
CHUNKS = 9
BF = jnp.bfloat16
F32 = jnp.float32
MESH = pl.DeviceIdType.MESH


def matmul_transposed(left, right):
    return lax.dot_general(left, right, (((1,), (1,)), ((), ())), preferred_element_type=F32)


def matmul(left, right):
    return jnp.dot(left, right, preferred_element_type=F32)


def depth_of(shape, axis):
    return lax.broadcasted_iota(jnp.int32, shape, axis) & (DEPTH - 1)


def rotated(values, step):
    turned = pltpu.roll(values.reshape(-1, 8, CH), step, 1)
    return turned.reshape(-1, 2, 8, CH)


def combined(wide, step, mirrored):
    first, middle, last = (wide[:, i * CH : (i + 1) * CH] for i in range(3))
    if mirrored:
        first, last = last, first
    depth = lax.broadcasted_iota(jnp.int32, (1, 8, CH), 1)
    low, high = depth < step, depth >= 8 - step
    down, up = rotated(first, step), rotated(last, 8 - step)
    upper = jnp.where(low, 0.0, down[:, 0]) + jnp.where(high, up[:, 1], up[:, 0])
    lower = jnp.where(low, down[:, 0], down[:, 1]) + jnp.where(high, 0.0, up[:, 1])
    return middle + jnp.stack([upper, lower], axis=1).reshape(-1, CH)


def store_transposed(target, slot, values, step):
    depth = depth_of((CH, CH), 1)
    for j in range(values.shape[0] // CH):
        block = jnp.transpose(values[j * CH : (j + 1) * CH, :])
        ahead = jnp.where(depth < DEPTH - step, pltpu.roll(block, CH - step, 1), 0.0)
        behind = jnp.where(depth >= step, pltpu.roll(block, step, 1), 0.0)
        columns = slice(j * CH, (j + 1) * CH)
        target[slot, 0:CH, columns] = ahead.astype(BF)
        target[slot, CH : 2 * CH, columns] = block.astype(BF)
        target[slot, 2 * CH : 3 * CH, columns] = behind.astype(BF)


def gates(values):
    sigma = 0.5 * jnp.tanh(0.5 * values) + 0.5
    return values * sigma, sigma * (1.0 + values * (1.0 - sigma))


def program(
    n_space,
    n_chan,
    feat,
    up,
    tiles,
    w1,
    w2,
    w3,
    coarse,
    out1,
    out2,
    out3,
    e1,
    e2,
    e3,
    e4,
    eu,
    d1,
    b2,
    v1f,
    v2f,
    v3f,
    v2b,
    v3b,
    st,
    gt,
    cf,
    raw_x,
    raw_up,
    wide,
    part,
    cs,
    cr,
    zs,
    zr,
    xs,
    xr,
    ys,
    yr,
    fs,
    fr,
    send_sem,
    recv_sem,
    local_sem,
):
    space = lax.axis_index("space")
    chan = lax.axis_index("chan")
    core = lax.rem(space, 2)
    chip_x = lax.rem(lax.div(space, 2), CHIPS)
    chip_y = lax.div(space, 2 * CHIPS)

    def near(d_space, d_chan):
        return (
            lax.rem(space + (d_space + n_space), n_space),
            lax.rem(chan + (d_chan + n_chan), n_chan),
        )

    sibling = (space + 1 - 2 * core, chan)

    def x_peer(d):
        return (chip_y * (2 * CHIPS) + lax.rem(chip_x + d, CHIPS) * 2 + core, chan)

    def y_peer(d):
        return (lax.rem(chip_y + d, CHIPS) * (2 * CHIPS) + chip_x * 2 + core, chan)

    started = []

    def send(source, target, device):
        index = len(started)
        copy = pltpu.make_async_remote_copy(
            src_ref=source,
            dst_ref=target,
            send_sem=send_sem.at[index],
            recv_sem=recv_sem.at[index],
            device_id=device,
            device_id_type=MESH,
        )
        copy.start()
        started.append(copy)
        return copy

    local = []

    def fetch(source, target):
        copy = pltpu.make_async_copy(source, target, local_sem.at[len(local)])
        copy.start()
        local.append(copy)
        return copy

    peers = [near(a, b) for a in (-1, 0, 1) for b in (-1, 0, 1) if (a, b) != (0, 0)]
    peers.append(near(0, 2))
    peers += [x_peer(d) for d in range(1, CHIPS)]
    peers += [y_peer(d) for d in range(1, CHIPS)]
    barrier = pltpu.get_barrier_semaphore()
    for peer in peers:
        pl.semaphore_signal(barrier, inc=1, device_id=peer, device_id_type=MESH)
    get_x = fetch(feat, raw_x)
    get_up = fetch(up, raw_up)

    def forward_weight(source, target):
        return [fetch(source.at[:, az], target.at[:, :, az]) for az in range(3)]

    def backward_weight(source, target):
        return [
            fetch(source.at[:, az], target.at[:, :, :, az * CH : (az + 1) * CH])
            for az in range(3)
        ]

    get_v1f = forward_weight(w1, v1f)
    get_v3b = backward_weight(w3, v3b)
    get_v2f = forward_weight(w2, v2f)
    get_v3f = forward_weight(w3, v3f)
    get_v2b = backward_weight(w2, v2b)

    def ready(copies):
        for copy in copies:
            copy.wait()

    get_x.wait()

    def turn(x, carry):
        for z in range(DEPTH):
            wide[pl.ds(z, LENGTH, stride=DEPTH), :] = raw_x[x, z].astype(F32)
        e1[1 + x, pl.ds(1, LENGTH)] = wide[...].astype(BF).reshape(LENGTH, DEPTH, CH)
        return carry

    lax.fori_loop(0, ROWS, turn, 0)
    get_up.wait()
    cf[...] = jnp.zeros_like(cf)
    for qx in range(2):
        for qz in range(DEPTH // 2):
            cf[pl.ds(2 * qz, HALF, stride=DEPTH), :] = raw_up[qx, qz].astype(F32)
        eu[qx, 0:HALF] = cf[...].astype(BF).reshape(HALF, DEPTH, CH)
    pl.semaphore_wait(barrier, len(peers))

    in_x, in_y = pl.ds(1, ROWS), pl.ds(1, LENGTH)
    top, right = ROWS, LENGTH
    sides = [
        send(e1.at[in_x, right], e1.at[in_x, 0], near(0, 1)),
        send(e1.at[in_x, 1], e1.at[in_x, right + 1], near(0, -1)),
    ]
    below = [
        send(e1.at[top, right], e1.at[0, 0], near(1, 1)),
        send(e1.at[top, 1], e1.at[0, right + 1], near(1, -1)),
        send(e1.at[top, in_y], e1.at[0, in_y], near(1, 0)),
    ]
    above = [
        send(e1.at[1, right], e1.at[top + 1, 0], near(-1, 1)),
        send(e1.at[1, 1], e1.at[top + 1, right + 1], near(-1, -1)),
        send(e1.at[1, in_y], e1.at[top + 1, in_y], near(-1, 0)),
    ]
    due_one = {0: below, 1: sides, 2: [], 3: [], 4: [], top + 1: above}
    halo_up = [
        send(eu.at[0, pl.ds(0, HALF)], eu.at[2, pl.ds(0, HALF)], near(-1, 0)),
        send(eu.at[pl.ds(0, 2), 0], eu.at[pl.ds(0, 2), HALF], near(0, -1)),
        send(eu.at[0, 0], eu.at[2, HALF], near(-1, -1)),
    ]

    def arrived(copies):
        for copy in copies:
            copy.wait_recv()

    def clear(ref, row, width):
        rows, columns = ref.shape[0], ref.shape[1]
        line = jnp.zeros((columns, DEPTH, CH), BF)
        corner = jnp.zeros((width, DEPTH, CH), BF)
        if row < width:

            @pl.when(space == 0)
            def _():
                ref[row] = line

        if row >= rows - width:

            @pl.when(space == n_space - 1)
            def _():
                ref[row] = line

        @pl.when(chan == 0)
        def _():
            ref[row, 0:width] = corner

        @pl.when(chan == n_chan - 1)
        def _():
            ref[row, columns - width : columns] = corner

    def need(ref, due, width, *rows):
        for row in rows:
            if row in due:
                arrived(due.pop(row))
                clear(ref, row, width)

    def spread_row(ref, due, x):
        own = x + 2
        far, to = (own + ROWS, -1) if x < 2 else (own - ROWS, 1)
        first, last, y = pl.ds(2, 2), pl.ds(LENGTH, 2), pl.ds(2, LENGTH)
        before, after = pl.ds(0, 2), pl.ds(LENGTH + 2, 2)
        due[own] = [
            send(ref.at[own, last], ref.at[own, before], near(0, 1)),
            send(ref.at[own, first], ref.at[own, after], near(0, -1)),
        ]
        due[far] = [
            send(ref.at[own, last], ref.at[far, before], near(to, 1)),
            send(ref.at[own, first], ref.at[far, after], near(to, -1)),
            send(ref.at[own, y], ref.at[far, y], near(to, 0)),
        ]

    def flat(block):
        return block.reshape(-1, CH)

    def window(ref, x, begin, spread):
        return jnp.concatenate(
            [
                flat(ref[x + spread * ax, pl.ds(begin + spread * ay, HALF)])
                for ax in range(3)
                for ay in range(3)
            ],
            axis=1,
        )

    def fluid(half):
        depth = lax.broadcasted_iota(jnp.int32, (DEPTH, CH), 0)
        column = jnp.zeros((DEPTH, CH), jnp.int32)
        for i in range(DEPTH // TILE_Z):
            column = jnp.where(lax.div(depth, TILE_Z) == i, tiles[0, half, i], column)
        cells = jnp.broadcast_to(column.astype(F32)[None], (HALF, DEPTH, CH))
        return flat(cells)

    def taps_of(weight):
        blocks = [weight[ax, ay].reshape(WIDE, CH) for ax in range(3) for ay in range(3)]
        return jnp.concatenate(blocks, axis=1)

    def over(low, high, step):
        def one(i, carry):
            step(lax.div(i, 2), lax.rem(i, 2))
            return carry

        lax.fori_loop(low, high, one, 0)

    for qx in range(2):
        store_transposed(gt, qx, flat(eu[qx, 0:HALF]).astype(F32), 1)

    ready(get_v1f)

    def layer_one(x, half):
        pre = combined(matmul_transposed(window(e1, x, half * HALF, 1), taps_of(v1f)), 1, False)
        hidden, slope = gates(pre)
        inside = fluid(half)
        block = (hidden * inside).astype(BF).reshape(HALF, DEPTH, CH)
        e2[2 + x, pl.ds(2 + half * HALF, HALF)] = block
        d1[x, half] = slope * inside

    due_two, due_four = {}, {}
    need(e1, due_one, 1, 1, 2, 3, 4)
    over(2, 6, layer_one)
    spread_row(e2, due_two, 1)
    spread_row(e2, due_two, 2)
    need(e1, due_one, 1, 0)
    over(0, 2, layer_one)
    spread_row(e2, due_two, 0)
    need(e1, due_one, 1, top + 1)
    over(6, 8, layer_one)
    spread_row(e2, due_two, 3)

    arrived(halo_up)
    ready(get_v3b)

    @pl.when(space == n_space - 1)
    def _():
        eu[2] = jnp.zeros((HALF + 1, DEPTH, CH), BF)

    @pl.when(chan == n_chan - 1)
    def _():
        eu[:, HALF] = jnp.zeros((3, DEPTH, CH), BF)

    routes = (((1, 0),), ((0, 1), (2, 0)))
    for qx in range(2):
        for px in range(2):
            for py in range(2):
                taps = [(ax, dx, ay, dy) for ax, dx in routes[px] for ay, dy in routes[py]]
                cells = [flat(eu[qx + dx, dy : dy + HALF]) for _, dx, _, dy in taps]
                rows = [v3b[ax, ay] for ax, _, ay, _ in taps]
                if len(taps) > 1:
                    cells, rows = [jnp.concatenate(cells, axis=1)], [jnp.concatenate(rows, axis=0)]
                back = combined(matmul(cells[0], rows[0]), 1, True)
                b2[2 * qx + px, py] = back.astype(BF).reshape(HALF, DEPTH, CH)

    ready(get_v2f)

    def layer_two(x, half):
        pre = combined(matmul_transposed(window(e2, x, half * HALF, 2), taps_of(v2f)), 2, False)
        hidden, slope = gates(pre)
        inside = fluid(half)
        pairs = (hidden * inside).astype(BF).reshape(HALF // 2, 2, DEPTH, CH)
        first = half * (HALF // 2)
        e3[1 + x, 1, pl.ds(first, HALF // 2)] = pairs[:, 0]
        e3[1 + x, 0, pl.ds(first + 1, HALF // 2)] = pairs[:, 1]
        back = [b2[x, r, pl.ds(first, HALF // 2)].astype(F32) for r in range(2)]
        back = flat(jnp.stack(back, axis=1))
        product = (back * inside * slope).astype(BF)
        e4[2 + x, pl.ds(2 + half * HALF, HALF)] = product.reshape(HALF, DEPTH, CH)
        store_transposed(st, 2 * x + half, product.astype(F32), 2)

    evens, odds = pl.ds(0, HALF), pl.ds(1, HALF)
    inner = pl.ds(1, ROWS)
    halo_three = []
    for x in (3, 2, 1, 0):
        need(e2, due_two, 2, x, x + 2, x + 4)
        over(2 * x, 2 * x + 2, layer_two)
        spread_row(e4, due_four, x)
        if x == 3:
            halo_three += [
                send(e3.at[ROWS, 0, HALF], e3.at[0, 0, 0], near(1, 1)),
                send(e3.at[ROWS, 1, evens], e3.at[0, 1, evens], near(1, 0)),
                send(e3.at[ROWS, 0, odds], e3.at[0, 0, odds], near(1, 0)),
            ]
    halo_three.append(send(e3.at[inner, 0, HALF], e3.at[inner, 0, 0], near(0, 1)))

    waits = {}

    def place(k):
        return k, slice(None)

    def share_core(k):
        b, w = place(k)
        cs[b, :, :, :, w] = part[b, :, :, 1 - core, :, w].astype(BF)
        waits[k] = [send(cs.at[b, :, :, :, w], cr.at[b, :, :, :, w], sibling)]

    def share_chan(k):
        b, w = place(k)
        arrived(waits[k])
        waits[k] = []
        for d in (2, 1, 3)[: n_chan - 1]:
            other = lax.rem(chan + d, n_chan)
            total = part[b, :, other, core, :, w] + cr[b, :, other, :, w].astype(F32)
            zs[b, d - 1, :, :, w] = total.astype(BF)
            block = (b, d - 1, slice(None), slice(None), w)
            waits[k].append(send(zs.at[block], zr.at[block], near(0, d)))

    def scatter(k, source, target, peer):
        b, w = place(k)
        waits[k] = [
            send(source.at[b, :, :, w], target.at[b, d - 1, :, :, w], peer(d)) for d in (2, 1, 3)
        ]

    def share_first(k):
        b, w = place(k)
        arrived(waits[k])
        total = part[b, :, chan, core, :, w] + cr[b, :, chan, :, w].astype(F32)
        for d in range(1, n_chan):
            total += zr[b, d - 1, :, :, w].astype(F32)
        xs[b, :, :, w] = total.astype(BF)
        scatter(k, xs, xr, (x_peer, y_peer)[k % 2])

    def four(own, others, k):
        b, w = place(k)
        opposite = own[b, :, :, w].astype(F32) + others[b, 1, :, :, w].astype(F32)
        return opposite + (others[b, 0, :, :, w].astype(F32) + others[b, 2, :, :, w].astype(F32))

    def share_second(k):
        b, w = place(k)
        arrived(waits[k])
        ys[b, :, :, w] = four(xs, xr, k).astype(BF)
        scatter(k, ys, yr, (y_peer, x_peer)[k % 2])

    def share_back(k):
        b, w = place(k)
        arrived(waits[k])
        fs[b, :, :, w] = four(ys, yr, k)
        waits[k] = [send(fs.at[b, :, :, w], fr.at[b, :, :, w], sibling)]

    def finish(k):
        b, _ = place(k)
        arrived(waits[k])
        out = (out2, out3, out1)[b // 3]
        for ay in range(3):
            columns = slice(ay * CH, (ay + 1) * CH)
            out[b % 3, :, ay, core] = fs[b, :, :, columns]
            out[b % 3, :, ay, 1 - core] = fr[b, :, :, columns]

    left = []

    def sent(keep):
        while len(left) < len(started) - keep:
            copy = started[len(left)]
            copy.wait_send()
            left.append(copy)

    stages = (share_core, share_chan, share_first, share_second, share_back, finish)
    progress = {}

    def advance(*chunks):
        for k in chunks:
            at = progress.get(k, 0)
            if at < len(stages):
                stages[at](k)
                progress[k] = at + 1

    def grads(k, ref, spread):
        ax = k % 3
        slopes = jnp.concatenate([st[i] for i in range(2 * ROWS)], axis=1)
        cells = jnp.concatenate(
            [
                jnp.concatenate(
                    [
                        flat(ref[x + spread * ax, spread * ay : spread * ay + LENGTH])
                        for ay in range(3)
                    ],
                    axis=1,
                )
                for x in range(ROWS)
            ],
            axis=0,
        )
        part[k] = matmul(slopes, cells).reshape(part.shape[1:])

    def coarse_window(x):
        return [flat(e3[x, r, j : j + HALF]) for r, j in ((0, 0), (1, 0), (0, 1))]

    def coarse_grads(k):
        ax = k % 3
        total = 0.0
        for qx in range(2):
            cells = jnp.concatenate(coarse_window(2 * qx + ax), axis=1)
            total += matmul(gt[qx], cells)
        part[k] = total.reshape(part.shape[1:])

    grads(0, e2, 2)
    advance(0)
    grads(1, e2, 2)
    advance(1)
    grads(2, e2, 2)
    advance(2, 0)
    arrived(halo_three)
    ready(get_v3f)

    @pl.when(space == 0)
    def _():
        e3[0] = jnp.zeros(e3.shape[1:], BF)

    @pl.when(chan == 0)
    def _():
        e3[:, 0, 0] = jnp.zeros((ROWS + 1, DEPTH, CH), BF)

    for k in range(3, 6):
        coarse_grads(k)
        advance(k)

    def coarse_rows(qx):
        cells = [block for ax in range(3) for block in coarse_window(2 * qx + ax)]
        cells = jnp.concatenate(cells, axis=1)
        cf[...] = combined(matmul_transposed(cells, taps_of(v3f)), 1, False)
        for qz in range(DEPTH // 2):
            coarse[qx, qz] = cf[pl.ds(2 * qz, HALF, stride=DEPTH), :].astype(BF)

    advance(1)
    ready(get_v2b)

    def layer_back(x, half):
        back = combined(matmul(mirror(x, half), v2b[...].reshape(TAPS, WIDE)), 2, True).astype(BF).astype(F32)
        slope = (back * d1[x, half]).astype(BF)
        store_transposed(st, 2 * x + half, slope.astype(F32), 1)

    def mirror(x, half):
        return jnp.concatenate(
            [
                flat(e4[x + 4 - 2 * ax, pl.ds(half * HALF + 4 - 2 * ay, HALF)])
                for ax in range(3)
                for ay in range(3)
            ],
            axis=1,
        )

    for x in (1, 0, 3, 2):
        need(e4, due_four, 2, x, x + 2, x + 4)
        over(2 * x, 2 * x + 2, layer_back)
        advance(*((2, 0) if x in (1, 3) else (3, 4, 5, 1)))
    grads(6, e1, 1)
    advance(6, 2, 0)
    grads(7, e1, 1)
    advance(7, 3, 4, 5)
    grads(8, e1, 1)
    advance(8, 6, 1)
    coarse_rows(0)
    advance(8, 7, 0, 2)
    coarse_rows(1)
    sent(60)
    advance(8, 6, 7)
    advance(3, 4, 5, 1, 2)
    sent(40)
    advance(8, 6, 7)
    advance(3, 4, 5)
    sent(24)
    advance(8, 6, 7)
    sent(12)
    advance(6, 7, 8)
    sent(0)
    assert all(progress[k] == len(stages) for k in range(CHUNKS))


def write_out(*refs):
    sources, targets, staged, sems = refs[:4], refs[4:8], refs[8:12], refs[12]
    loads = [
        pltpu.make_async_copy(a, b, sems.at[i]) for i, (a, b) in enumerate(zip(sources, staged))
    ]
    stores = [
        pltpu.make_async_copy(a, b, sems.at[4 + i]) for i, (a, b) in enumerate(zip(staged, targets))
    ]
    for copy in loads:
        copy.start()
    for load, store in zip(loads, stores):
        load.wait()
        store.start()
    for copy in stores:
        copy.wait()


def local(features, fluid_tiles, weight_one, weight_two, weight_three, upstream, sizes):
    n_space, n_chan = sizes
    tiles = jnp.transpose(fluid_tiles, (0, 2, 1))

    def by_tap(weight):
        return jnp.transpose(weight, (1, 2, 3, 0, 4))

    def by_output(grad):
        return jnp.transpose(grad.reshape(3, 3, 3, 2 * 16, CH), (3, 0, 1, 2, 4))

    hbm = pl.BlockSpec(memory_space=pl.ANY)
    vmem = pl.BlockSpec(memory_space=pltpu.VMEM)
    smem = pl.BlockSpec(memory_space=pltpu.SMEM)
    grad_shape = jax.ShapeDtypeStruct((3, 3, 3, 2, 16, CH), F32)
    copies = 55 + 11 * (CHUNKS)
    forward_shape = pltpu.VMEM((3, 3, 3, CH, CH), BF)
    backward_shape = pltpu.VMEM((3, 3, CH, WIDE), BF)
    piece = (CHUNKS, 3, 16, WIDE)
    pieces = (CHUNKS, 3, 3, 16, WIDE)
    results = pl.pallas_call(
        functools.partial(program, n_space, n_chan),
        out_shape=(
            jax.ShapeDtypeStruct((2, DEPTH // 2, HALF, CH), BF),
            grad_shape,
            grad_shape,
            grad_shape,
        ),
        in_specs=[hbm, hbm, smem, hbm, hbm, hbm],
        out_specs=[vmem] * 4,
        scratch_shapes=[
            pltpu.VMEM((ROWS + 2, LENGTH + 2, DEPTH, CH), BF),
            pltpu.VMEM((ROWS + 4, LENGTH + 4, DEPTH, CH), BF),
            pltpu.VMEM((ROWS + 1, 2, HALF + 1, DEPTH, CH), BF),
            pltpu.VMEM((ROWS + 4, LENGTH + 4, DEPTH, CH), BF),
            pltpu.VMEM((3, HALF + 1, DEPTH, CH), BF),
            pltpu.VMEM((ROWS, 2, CELLS, CH), F32),
            pltpu.VMEM((ROWS, 2, HALF, DEPTH, CH), BF),
            forward_shape,
            forward_shape,
            forward_shape,
            backward_shape,
            backward_shape,
            pltpu.VMEM((8, WIDE, CELLS), BF),
            pltpu.VMEM((2, WIDE, CELLS), BF),
            pltpu.VMEM((CELLS, CH), F32),
            pltpu.VMEM((ROWS, DEPTH, LENGTH, CH), BF),
            pltpu.VMEM((2, DEPTH // 2, HALF, CH), BF),
            pltpu.VMEM((LENGTH * DEPTH, CH), F32),
            pltpu.VMEM((CHUNKS, 3, n_chan, 2, 16, WIDE), F32),
            pltpu.VMEM((CHUNKS, 3, n_chan, 16, WIDE), BF),
            pltpu.VMEM((CHUNKS, 3, n_chan, 16, WIDE), BF),
            pltpu.VMEM(pieces, BF),
            pltpu.VMEM(pieces, BF),
            pltpu.VMEM(piece, BF),
            pltpu.VMEM(pieces, BF),
            pltpu.VMEM(piece, BF),
            pltpu.VMEM(pieces, BF),
            pltpu.VMEM(piece, F32),
            pltpu.VMEM(piece, F32),
            pltpu.SemaphoreType.DMA((copies,)),
            pltpu.SemaphoreType.DMA((copies,)),
            pltpu.SemaphoreType.DMA((17,)),
        ],
        compiler_params=pltpu.CompilerParams(
            collective_id=0, has_side_effects=True, vmem_limit_bytes=58 << 20
        ),
    )(
        features,
        upstream,
        tiles,
        by_tap(weight_one),
        by_tap(weight_two),
        by_tap(weight_three),
    )
    coarse, grad_one, grad_two, grad_three = pl.pallas_call(
        write_out,
        out_shape=tuple(jax.ShapeDtypeStruct(r.shape, r.dtype) for r in results),
        in_specs=[hbm] * 4,
        out_specs=[hbm] * 4,
        scratch_shapes=[pltpu.VMEM(r.shape, r.dtype) for r in results]
        + [pltpu.SemaphoreType.DMA((8,))],
    )(*results)
    return coarse, by_output(grad_one), by_output(grad_two), by_output(grad_three)


def solution(mesh):
    in_specs = (
        P("space", None, "chan", None),
        P("space", None, "chan"),
        P(),
        P(),
        P(),
        P("space", None, "chan", None),
    )
    out_specs = (
        P("space", None, "chan", None),
        P("chan", None, None, None, None),
        P("chan", None, None, None, None),
        P("chan", None, None, None, None),
    )
    sizes = (mesh.shape["space"], mesh.shape["chan"])
    return jax.shard_map(
        functools.partial(local, sizes=sizes),
        mesh=mesh,
        in_specs=in_specs,
        out_specs=out_specs,
        check_vma=False,
    )
```

```python
import functools

import jax
import jax.numpy as jnp
from jax import lax
from jax.experimental import pallas as pl
from jax.experimental.pallas import tpu as pltpu
from jax.sharding import PartitionSpec as P

TILE_Z = 4
TILE_Y = 32
ROWS = 4
LENGTH = 64
DEPTH = 16
CH = 128
HALF = LENGTH // 2
CELLS = HALF * DEPTH
TAPS = 9 * CH
WIDE = 3 * CH
CHIPS = 4
CHUNKS = 9
BF = jnp.bfloat16
F32 = jnp.float32
MESH = pl.DeviceIdType.MESH


def matmul_transposed(left, right):
    return lax.dot_general(left, right, (((1,), (1,)), ((), ())), preferred_element_type=F32)


def matmul(left, right):
    return jnp.dot(left, right, preferred_element_type=F32)


def depth_of(shape, axis):
    return lax.broadcasted_iota(jnp.int32, shape, axis) & (DEPTH - 1)


def rotated(values, step):
    turned = pltpu.roll(values.reshape(-1, 8, CH), step, 1)
    return turned.reshape(-1, 2, 8, CH)


def combined(wide, step, mirrored):
    first, middle, last = (wide[:, i * CH : (i + 1) * CH] for i in range(3))
    if mirrored:
        first, last = last, first
    depth = lax.broadcasted_iota(jnp.int32, (1, 8, CH), 1)
    low, high = depth < step, depth >= 8 - step
    down, up = rotated(first, step), rotated(last, 8 - step)
    upper = jnp.where(low, 0.0, down[:, 0]) + jnp.where(high, up[:, 1], up[:, 0])
    lower = jnp.where(low, down[:, 0], down[:, 1]) + jnp.where(high, 0.0, up[:, 1])
    return middle + jnp.stack([upper, lower], axis=1).reshape(-1, CH)


def store_transposed(target, slot, values, step):
    depth = depth_of((CH, CH), 1)
    for j in range(values.shape[0] // CH):
        block = jnp.transpose(values[j * CH : (j + 1) * CH, :])
        ahead = jnp.where(depth < DEPTH - step, pltpu.roll(block, CH - step, 1), 0.0)
        behind = jnp.where(depth >= step, pltpu.roll(block, step, 1), 0.0)
        columns = slice(j * CH, (j + 1) * CH)
        target[slot, 0:CH, columns] = ahead.astype(BF)
        target[slot, CH : 2 * CH, columns] = block.astype(BF)
        target[slot, 2 * CH : 3 * CH, columns] = behind.astype(BF)


def gates(values):
    sigma = 0.5 * jnp.tanh(0.5 * values) + 0.5
    return values * sigma, sigma * (1.0 + values * (1.0 - sigma))


def program(
    n_space,
    n_chan,
    feat,
    up,
    tiles,
    w1,
    w2,
    w3,
    coarse,
    out1,
    out2,
    out3,
    e1,
    e2,
    e3,
    e4,
    eu,
    d1,
    b2,
    v1f,
    v2f,
    v3f,
    v2b,
    v3b,
    st,
    gt,
    cf,
    raw_x,
    raw_up,
    wide,
    part,
    cs,
    cr,
    zs,
    zr,
    xs,
    xr,
    ys,
    yr,
    fs,
    fr,
    send_sem,
    recv_sem,
    local_sem,
):
    space = lax.axis_index("space")
    chan = lax.axis_index("chan")
    core = lax.rem(space, 2)
    chip_x = lax.rem(lax.div(space, 2), CHIPS)
    chip_y = lax.div(space, 2 * CHIPS)

    def near(d_space, d_chan):
        return (
            lax.rem(space + (d_space + n_space), n_space),
            lax.rem(chan + (d_chan + n_chan), n_chan),
        )

    sibling = (space + 1 - 2 * core, chan)

    def x_peer(d):
        return (chip_y * (2 * CHIPS) + lax.rem(chip_x + d, CHIPS) * 2 + core, chan)

    def y_peer(d):
        return (lax.rem(chip_y + d, CHIPS) * (2 * CHIPS) + chip_x * 2 + core, chan)

    started = []

    def send(source, target, device):
        index = len(started)
        copy = pltpu.make_async_remote_copy(
            src_ref=source,
            dst_ref=target,
            send_sem=send_sem.at[index],
            recv_sem=recv_sem.at[index],
            device_id=device,
            device_id_type=MESH,
        )
        copy.start()
        started.append(copy)
        return copy

    local = []

    def fetch(source, target):
        copy = pltpu.make_async_copy(source, target, local_sem.at[len(local)])
        copy.start()
        local.append(copy)
        return copy

    peers = [near(a, b) for a in (-1, 0, 1) for b in (-1, 0, 1) if (a, b) != (0, 0)]
    peers.append(near(0, 2))
    peers += [x_peer(d) for d in range(1, CHIPS)]
    peers += [y_peer(d) for d in range(1, CHIPS)]
    barrier = pltpu.get_barrier_semaphore()
    for peer in peers:
        pl.semaphore_signal(barrier, inc=1, device_id=peer, device_id_type=MESH)
    get_x = fetch(feat, raw_x)
    get_up = fetch(up, raw_up)

    def forward_weight(source, target):
        return [fetch(source.at[:, az], target.at[:, :, az]) for az in range(3)]

    def backward_weight(source, target):
        return [
            fetch(source.at[:, az], target.at[:, :, :, az * CH : (az + 1) * CH])
            for az in range(3)
        ]

    get_v1f = forward_weight(w1, v1f)
    get_v3b = backward_weight(w3, v3b)
    get_v2f = forward_weight(w2, v2f)
    get_v3f = forward_weight(w3, v3f)
    get_v2b = backward_weight(w2, v2b)

    def ready(copies):
        for copy in copies:
            copy.wait()

    get_x.wait()

    def turn(x, carry):
        for z in range(DEPTH):
            wide[pl.ds(z, LENGTH, stride=DEPTH), :] = raw_x[x, z].astype(F32)
        e1[1 + x, pl.ds(1, LENGTH)] = wide[...].astype(BF).reshape(LENGTH, DEPTH, CH)
        return carry

    lax.fori_loop(0, ROWS, turn, 0)
    get_up.wait()
    cf[...] = jnp.zeros_like(cf)
    for qx in range(2):
        for qz in range(DEPTH // 2):
            cf[pl.ds(2 * qz, HALF, stride=DEPTH), :] = raw_up[qx, qz].astype(F32)
        eu[qx, 0:HALF] = cf[...].astype(BF).reshape(HALF, DEPTH, CH)
    pl.semaphore_wait(barrier, len(peers))

    in_x, in_y = pl.ds(1, ROWS), pl.ds(1, LENGTH)
    top, right = ROWS, LENGTH
    sides = [
        send(e1.at[in_x, right], e1.at[in_x, 0], near(0, 1)),
        send(e1.at[in_x, 1], e1.at[in_x, right + 1], near(0, -1)),
    ]
    below = [
        send(e1.at[top, right], e1.at[0, 0], near(1, 1)),
        send(e1.at[top, 1], e1.at[0, right + 1], near(1, -1)),
        send(e1.at[top, in_y], e1.at[0, in_y], near(1, 0)),
    ]
    above = [
        send(e1.at[1, right], e1.at[top + 1, 0], near(-1, 1)),
        send(e1.at[1, 1], e1.at[top + 1, right + 1], near(-1, -1)),
        send(e1.at[1, in_y], e1.at[top + 1, in_y], near(-1, 0)),
    ]
    due_one = {0: below, 1: sides, 2: [], 3: [], 4: [], top + 1: above}
    halo_up = [
        send(eu.at[0, pl.ds(0, HALF)], eu.at[2, pl.ds(0, HALF)], near(-1, 0)),
        send(eu.at[pl.ds(0, 2), 0], eu.at[pl.ds(0, 2), HALF], near(0, -1)),
        send(eu.at[0, 0], eu.at[2, HALF], near(-1, -1)),
    ]

    def arrived(copies):
        for copy in copies:
            copy.wait_recv()

    def clear(ref, row, width):
        rows, columns = ref.shape[0], ref.shape[1]
        line = jnp.zeros((columns, DEPTH, CH), BF)
        corner = jnp.zeros((width, DEPTH, CH), BF)
        if row < width:

            @pl.when(space == 0)
            def _():
                ref[row] = line

        if row >= rows - width:

            @pl.when(space == n_space - 1)
            def _():
                ref[row] = line

        @pl.when(chan == 0)
        def _():
            ref[row, 0:width] = corner

        @pl.when(chan == n_chan - 1)
        def _():
            ref[row, columns - width : columns] = corner

    def need(ref, due, width, *rows):
        for row in rows:
            if row in due:
                arrived(due.pop(row))
                clear(ref, row, width)

    def spread_row(ref, due, x):
        own = x + 2
        far, to = (own + ROWS, -1) if x < 2 else (own - ROWS, 1)
        first, last, y = pl.ds(2, 2), pl.ds(LENGTH, 2), pl.ds(2, LENGTH)
        before, after = pl.ds(0, 2), pl.ds(LENGTH + 2, 2)
        due[own] = [
            send(ref.at[own, last], ref.at[own, before], near(0, 1)),
            send(ref.at[own, first], ref.at[own, after], near(0, -1)),
        ]
        due[far] = [
            send(ref.at[own, last], ref.at[far, before], near(to, 1)),
            send(ref.at[own, first], ref.at[far, after], near(to, -1)),
            send(ref.at[own, y], ref.at[far, y], near(to, 0)),
        ]

    def flat(block):
        return block.reshape(-1, CH)

    def window(ref, x, begin, spread):
        return jnp.concatenate(
            [
                flat(ref[x + spread * ax, pl.ds(begin + spread * ay, HALF)])
                for ax in range(3)
                for ay in range(3)
            ],
            axis=1,
        )

    def fluid(half):
        depth = lax.broadcasted_iota(jnp.int32, (DEPTH, CH), 0)
        column = jnp.zeros((DEPTH, CH), jnp.int32)
        for i in range(DEPTH // TILE_Z):
            column = jnp.where(lax.div(depth, TILE_Z) == i, tiles[0, half, i], column)
        cells = jnp.broadcast_to(column.astype(F32)[None], (HALF, DEPTH, CH))
        return flat(cells)

    def taps_of(weight):
        blocks = [weight[ax, ay].reshape(WIDE, CH) for ax in range(3) for ay in range(3)]
        return jnp.concatenate(blocks, axis=1)

    def over(low, high, step):
        def one(i, carry):
            step(lax.div(i, 2), lax.rem(i, 2))
            return carry

        lax.fori_loop(low, high, one, 0)

    for qx in range(2):
        store_transposed(gt, qx, flat(eu[qx, 0:HALF]).astype(F32), 1)

    ready(get_v1f)

    def layer_one(x, half):
        pre = combined(matmul_transposed(window(e1, x, half * HALF, 1), taps_of(v1f)), 1, False)
        hidden, slope = gates(pre)
        inside = fluid(half)
        block = (hidden * inside).astype(BF).reshape(HALF, DEPTH, CH)
        e2[2 + x, pl.ds(2 + half * HALF, HALF)] = block
        d1[x, half] = slope * inside

    due_two, due_four = {}, {}
    need(e1, due_one, 1, 1, 2, 3, 4)
    over(2, 6, layer_one)
    spread_row(e2, due_two, 1)
    spread_row(e2, due_two, 2)
    need(e1, due_one, 1, 0)
    over(0, 2, layer_one)
    spread_row(e2, due_two, 0)
    need(e1, due_one, 1, top + 1)
    over(6, 8, layer_one)
    spread_row(e2, due_two, 3)

    arrived(halo_up)
    ready(get_v3b)

    @pl.when(space == n_space - 1)
    def _():
        eu[2] = jnp.zeros((HALF + 1, DEPTH, CH), BF)

    @pl.when(chan == n_chan - 1)
    def _():
        eu[:, HALF] = jnp.zeros((3, DEPTH, CH), BF)

    routes = (((1, 0),), ((0, 1), (2, 0)))
    for qx in range(2):
        for px in range(2):
            for py in range(2):
                taps = [(ax, dx, ay, dy) for ax, dx in routes[px] for ay, dy in routes[py]]
                cells = [flat(eu[qx + dx, dy : dy + HALF]) for _, dx, _, dy in taps]
                rows = [v3b[ax, ay] for ax, _, ay, _ in taps]
                if len(taps) > 1:
                    cells, rows = [jnp.concatenate(cells, axis=1)], [jnp.concatenate(rows, axis=0)]
                back = combined(matmul(cells[0], rows[0]), 1, True)
                b2[2 * qx + px, py] = back.astype(BF).reshape(HALF, DEPTH, CH)

    ready(get_v2f)

    def layer_two(x, half):
        pre = combined(matmul_transposed(window(e2, x, half * HALF, 2), taps_of(v2f)), 2, False)
        hidden, slope = gates(pre)
        inside = fluid(half)
        pairs = (hidden * inside).astype(BF).reshape(HALF // 2, 2, DEPTH, CH)
        first = half * (HALF // 2)
        e3[1 + x, 1, pl.ds(first, HALF // 2)] = pairs[:, 0]
        e3[1 + x, 0, pl.ds(first + 1, HALF // 2)] = pairs[:, 1]
        back = [b2[x, r, pl.ds(first, HALF // 2)].astype(F32) for r in range(2)]
        back = flat(jnp.stack(back, axis=1))
        product = (back * inside * slope).astype(BF)
        e4[2 + x, pl.ds(2 + half * HALF, HALF)] = product.reshape(HALF, DEPTH, CH)
        store_transposed(st, 2 * x + half, product.astype(F32), 2)

    evens, odds = pl.ds(0, HALF), pl.ds(1, HALF)
    inner = pl.ds(1, ROWS)
    halo_three = []
    for x in (3, 2, 1, 0):
        need(e2, due_two, 2, x, x + 2, x + 4)
        over(2 * x, 2 * x + 2, layer_two)
        spread_row(e4, due_four, x)
        if x == 3:
            halo_three += [
                send(e3.at[ROWS, 0, HALF], e3.at[0, 0, 0], near(1, 1)),
                send(e3.at[ROWS, 1, evens], e3.at[0, 1, evens], near(1, 0)),
                send(e3.at[ROWS, 0, odds], e3.at[0, 0, odds], near(1, 0)),
            ]
    halo_three.append(send(e3.at[inner, 0, HALF], e3.at[inner, 0, 0], near(0, 1)))

    waits = {}

    def place(k):
        return k, slice(None)

    def share_core(k):
        b, w = place(k)
        cs[b, :, :, :, w] = part[b, :, :, 1 - core, :, w].astype(BF)
        waits[k] = [send(cs.at[b, :, :, :, w], cr.at[b, :, :, :, w], sibling)]

    def share_chan(k):
        b, w = place(k)
        arrived(waits[k])
        waits[k] = []
        for d in (2, 1, 3)[: n_chan - 1]:
            other = lax.rem(chan + d, n_chan)
            total = part[b, :, other, core, :, w] + cr[b, :, other, :, w].astype(F32)
            zs[b, d - 1, :, :, w] = total.astype(BF)
            block = (b, d - 1, slice(None), slice(None), w)
            waits[k].append(send(zs.at[block], zr.at[block], near(0, d)))

    def scatter(k, source, target, peer):
        b, w = place(k)
        waits[k] = [
            send(source.at[b, :, :, w], target.at[b, d - 1, :, :, w], peer(d)) for d in (2, 1, 3)
        ]

    def share_first(k):
        b, w = place(k)
        arrived(waits[k])
        total = part[b, :, chan, core, :, w] + cr[b, :, chan, :, w].astype(F32)
        for d in range(1, n_chan):
            total += zr[b, d - 1, :, :, w].astype(F32)
        xs[b, :, :, w] = total.astype(BF)
        scatter(k, xs, xr, (x_peer, y_peer)[k % 2])

    def four(own, others, k):
        b, w = place(k)
        opposite = own[b, :, :, w].astype(F32) + others[b, 1, :, :, w].astype(F32)
        return opposite + (others[b, 0, :, :, w].astype(F32) + others[b, 2, :, :, w].astype(F32))

    def share_second(k):
        b, w = place(k)
        arrived(waits[k])
        ys[b, :, :, w] = four(xs, xr, k).astype(BF)
        scatter(k, ys, yr, (y_peer, x_peer)[k % 2])

    def share_back(k):
        b, w = place(k)
        arrived(waits[k])
        fs[b, :, :, w] = four(ys, yr, k)
        waits[k] = [send(fs.at[b, :, :, w], fr.at[b, :, :, w], sibling)]

    def finish(k):
        b, _ = place(k)
        arrived(waits[k])
        out = (out2, out3, out1)[b // 3]
        for ay in range(3):
            columns = slice(ay * CH, (ay + 1) * CH)
            out[b % 3, :, ay, core] = fs[b, :, :, columns]
            out[b % 3, :, ay, 1 - core] = fr[b, :, :, columns]

    left = []

    def sent(keep):
        while len(left) < len(started) - keep:
            copy = started[len(left)]
            copy.wait_send()
            left.append(copy)

    stages = (share_core, share_chan, share_first, share_second, share_back, finish)
    progress = {}

    def advance(*chunks):
        for k in chunks:
            at = progress.get(k, 0)
            if at < len(stages):
                stages[at](k)
                progress[k] = at + 1

    def grads(k, ref, spread):
        ax = k % 3
        slopes = jnp.concatenate([st[i] for i in range(2 * ROWS)], axis=1)
        cells = jnp.concatenate(
            [
                jnp.concatenate(
                    [
                        flat(ref[x + spread * ax, spread * ay : spread * ay + LENGTH])
                        for ay in range(3)
                    ],
                    axis=1,
                )
                for x in range(ROWS)
            ],
            axis=0,
        )
        part[k] = matmul(slopes, cells).reshape(part.shape[1:])

    def coarse_window(x):
        return [flat(e3[x, r, j : j + HALF]) for r, j in ((0, 0), (1, 0), (0, 1))]

    def coarse_grads(k):
        ax = k % 3
        total = 0.0
        for qx in range(2):
            cells = jnp.concatenate(coarse_window(2 * qx + ax), axis=1)
            total += matmul(gt[qx], cells)
        part[k] = total.reshape(part.shape[1:])

    grads(0, e2, 2)
    advance(0)
    grads(1, e2, 2)
    advance(1)
    grads(2, e2, 2)
    advance(2, 0)
    arrived(halo_three)
    ready(get_v3f)

    @pl.when(space == 0)
    def _():
        e3[0] = jnp.zeros(e3.shape[1:], BF)

    @pl.when(chan == 0)
    def _():
        e3[:, 0, 0] = jnp.zeros((ROWS + 1, DEPTH, CH), BF)

    for k in range(3, 6):
        coarse_grads(k)
        advance(k)

    def coarse_rows(qx):
        cells = [block for ax in range(3) for block in coarse_window(2 * qx + ax)]
        cells = jnp.concatenate(cells, axis=1)
        cf[...] = combined(matmul_transposed(cells, taps_of(v3f)), 1, False)
        for qz in range(DEPTH // 2):
            coarse[qx, qz] = cf[pl.ds(2 * qz, HALF, stride=DEPTH), :].astype(BF)

    advance(1)
    ready(get_v2b)

    def layer_back(x, half):
        back = combined(matmul(mirror(x, half), v2b[...].reshape(TAPS, WIDE)), 2, True).astype(BF).astype(F32)
        slope = (back * d1[x, half]).astype(BF)
        store_transposed(st, 2 * x + half, slope.astype(F32), 1)

    def mirror(x, half):
        return jnp.concatenate(
            [
                flat(e4[x + 4 - 2 * ax, pl.ds(half * HALF + 4 - 2 * ay, HALF)])
                for ax in range(3)
                for ay in range(3)
            ],
            axis=1,
        )

    for x in (1, 0, 3, 2):
        need(e4, due_four, 2, x, x + 2, x + 4)
        over(2 * x, 2 * x + 2, layer_back)
        advance(*((2, 0) if x in (1, 3) else (3, 4, 5, 1)))
    grads(6, e1, 1)
    advance(6, 2, 0)
    grads(7, e1, 1)
    advance(7, 3, 4, 5)
    grads(8, e1, 1)
    advance(8, 6, 1)
    coarse_rows(0)
    advance(7, 0, 2, 8)
    coarse_rows(1)
    sent(60)
    advance(8, 6, 7)
    advance(3, 4, 5, 1, 2)
    sent(40)
    advance(8, 6, 7)
    advance(3, 4, 5)
    sent(24)
    advance(8, 6, 7)
    sent(12)
    advance(6, 7, 8)
    sent(0)
    assert all(progress[k] == len(stages) for k in range(CHUNKS))


def write_out(*refs):
    sources, targets, staged, sems = refs[:4], refs[4:8], refs[8:12], refs[12]
    loads = [
        pltpu.make_async_copy(a, b, sems.at[i]) for i, (a, b) in enumerate(zip(sources, staged))
    ]
    stores = [
        pltpu.make_async_copy(a, b, sems.at[4 + i]) for i, (a, b) in enumerate(zip(staged, targets))
    ]
    for copy in loads:
        copy.start()
    for load, store in zip(loads, stores):
        load.wait()
        store.start()
    for copy in stores:
        copy.wait()


def local(features, fluid_tiles, weight_one, weight_two, weight_three, upstream, sizes):
    n_space, n_chan = sizes
    tiles = jnp.transpose(fluid_tiles, (0, 2, 1))

    def by_tap(weight):
        return jnp.transpose(weight, (1, 2, 3, 0, 4))

    def by_output(grad):
        return jnp.transpose(grad.reshape(3, 3, 3, 2 * 16, CH), (3, 0, 1, 2, 4))

    hbm = pl.BlockSpec(memory_space=pl.ANY)
    vmem = pl.BlockSpec(memory_space=pltpu.VMEM)
    smem = pl.BlockSpec(memory_space=pltpu.SMEM)
    grad_shape = jax.ShapeDtypeStruct((3, 3, 3, 2, 16, CH), F32)
    copies = 55 + 11 * (CHUNKS)
    forward_shape = pltpu.VMEM((3, 3, 3, CH, CH), BF)
    backward_shape = pltpu.VMEM((3, 3, CH, WIDE), BF)
    piece = (CHUNKS, 3, 16, WIDE)
    pieces = (CHUNKS, 3, 3, 16, WIDE)
    results = pl.pallas_call(
        functools.partial(program, n_space, n_chan),
        out_shape=(
            jax.ShapeDtypeStruct((2, DEPTH // 2, HALF, CH), BF),
            grad_shape,
            grad_shape,
            grad_shape,
        ),
        in_specs=[hbm, hbm, smem, hbm, hbm, hbm],
        out_specs=[vmem] * 4,
        scratch_shapes=[
            pltpu.VMEM((ROWS + 2, LENGTH + 2, DEPTH, CH), BF),
            pltpu.VMEM((ROWS + 4, LENGTH + 4, DEPTH, CH), BF),
            pltpu.VMEM((ROWS + 1, 2, HALF + 1, DEPTH, CH), BF),
            pltpu.VMEM((ROWS + 4, LENGTH + 4, DEPTH, CH), BF),
            pltpu.VMEM((3, HALF + 1, DEPTH, CH), BF),
            pltpu.VMEM((ROWS, 2, CELLS, CH), F32),
            pltpu.VMEM((ROWS, 2, HALF, DEPTH, CH), BF),
            forward_shape,
            forward_shape,
            forward_shape,
            backward_shape,
            backward_shape,
            pltpu.VMEM((8, WIDE, CELLS), BF),
            pltpu.VMEM((2, WIDE, CELLS), BF),
            pltpu.VMEM((CELLS, CH), F32),
            pltpu.VMEM((ROWS, DEPTH, LENGTH, CH), BF),
            pltpu.VMEM((2, DEPTH // 2, HALF, CH), BF),
            pltpu.VMEM((LENGTH * DEPTH, CH), F32),
            pltpu.VMEM((CHUNKS, 3, n_chan, 2, 16, WIDE), F32),
            pltpu.VMEM((CHUNKS, 3, n_chan, 16, WIDE), BF),
            pltpu.VMEM((CHUNKS, 3, n_chan, 16, WIDE), BF),
            pltpu.VMEM(pieces, BF),
            pltpu.VMEM(pieces, BF),
            pltpu.VMEM(piece, BF),
            pltpu.VMEM(pieces, BF),
            pltpu.VMEM(piece, BF),
            pltpu.VMEM(pieces, BF),
            pltpu.VMEM(piece, F32),
            pltpu.VMEM(piece, F32),
            pltpu.SemaphoreType.DMA((copies,)),
            pltpu.SemaphoreType.DMA((copies,)),
            pltpu.SemaphoreType.DMA((17,)),
        ],
        compiler_params=pltpu.CompilerParams(
            collective_id=0, has_side_effects=True, vmem_limit_bytes=58 << 20
        ),
    )(
        features,
        upstream,
        tiles,
        by_tap(weight_one),
        by_tap(weight_two),
        by_tap(weight_three),
    )
    coarse, grad_one, grad_two, grad_three = pl.pallas_call(
        write_out,
        out_shape=tuple(jax.ShapeDtypeStruct(r.shape, r.dtype) for r in results),
        in_specs=[hbm] * 4,
        out_specs=[hbm] * 4,
        scratch_shapes=[pltpu.VMEM(r.shape, r.dtype) for r in results]
        + [pltpu.SemaphoreType.DMA((8,))],
    )(*results)
    return coarse, by_output(grad_one), by_output(grad_two), by_output(grad_three)


def solution(mesh):
    in_specs = (
        P("space", None, "chan", None),
        P("space", None, "chan"),
        P(),
        P(),
        P(),
        P("space", None, "chan", None),
    )
    out_specs = (
        P("space", None, "chan", None),
        P("chan", None, None, None, None),
        P("chan", None, None, None, None),
        P("chan", None, None, None, None),
    )
    sizes = (mesh.shape["space"], mesh.shape["chan"])
    return jax.shard_map(
        functools.partial(local, sizes=sizes),
        mesh=mesh,
        in_specs=in_specs,
        out_specs=out_specs,
        check_vma=False,
    )
```
